32 devices in a mesh: row: 4 (over z), col: 4 (over x, core), layer: 2 (over y).
Axes of the slice: x: 2, y: 2, z: 4, core: 2. Of those that a mesh axis runs over, the one named last changes fastest.
Arguments:
- left_blocks: float32 [4, 2, 4, 4, 128, 128], P('row', 'layer', 'col'), may hold values from -1.2 to 1.2
- right_blocks: float32 [2, 4, 4, 8, 128, 128], P('layer', 'row', 'col'), may hold values from -1.2 to 1.2
- pair_stacks: int32 [4, 4, 2, 4, 3, 32], P('row', 'col', 'layer'), may hold values from 0 to 32, as said below
Outputs:
- product_window: float32 [4, 4, 32, 128, 128], P('row', 'col', 'layer')
The draws below stay inside these ranges and needn't reach their ends.
Inputs may be any that keep to these rules, and one draw needn't show every extreme that they name: `pair_stacks`: entry 0 of a list holds left slots below 4, entry 1 right slots below 8, entry 2 product blocks below 32; the live triples stand first, every other slot holds (0, 0, 32); some list is live in all 32 slots.
All inputs are finite; a program needn't handle non-finite values.
Results may differ from the reference program's by a relative error of at most 0.0003.
Values sent between devices are 32-bit elements; how exact they have to be, the bound alone decides.
A program may use at most 64 MiB of HBM per device.

```python
import jax
import jax.numpy as jnp
from jax import lax

BS = 128
SA = 4
SB = 8
PCAP = 32
OUT_TILE = 32
ROW_TILES = 4
COL_TILES = 4
K_PARTS = 2
PIECES = 4


def draw_pair_stacks(key, part):
    grid_shape = (ROW_TILES, COL_TILES, K_PARTS, PIECES)
    key_tile, key_piece, key_chosen, key_left, key_right, key_out = jax.random.split(key, 6)
    tile_load = jax.random.randint(key_tile, (ROW_TILES, COL_TILES, 1, 1), 8, 33)
    piece_load = jax.random.randint(key_piece, grid_shape, 24, 33)
    live_counts = PCAP * tile_load * piece_load // 1024
    flat_loads = live_counts.reshape(-1)
    chosen = jax.random.randint(key_chosen, (), 0, flat_loads.shape[0])
    flat_loads = jnp.where(jnp.arange(flat_loads.shape[0]) == chosen, PCAP, flat_loads)
    live_counts = flat_loads.reshape(grid_shape)
    slot_ids = jnp.arange(PCAP)
    live_mask = slot_ids < live_counts[..., None]
    left_slot = jax.random.randint(key_left, grid_shape + (PCAP,), 0, SA)
    right_slot = jax.random.randint(key_right, grid_shape + (PCAP,), 0, SB)
    out_slot = jax.random.randint(key_out, grid_shape + (PCAP,), 0, OUT_TILE)
    left_slot = jnp.where(live_mask, left_slot, 0)
    right_slot = jnp.where(live_mask, right_slot, 0)
    out_slot = jnp.where(live_mask, out_slot, OUT_TILE)
    return jnp.stack([left_slot, right_slot, out_slot], axis=-2).astype(jnp.int32)


def level_of(own_key, shape, cuts, least, high):
    gain = 1.0
    for axis_at, shards_of in cuts:
        draws = jax.random.uniform(jax.random.fold_in(jax.random.fold_in(own_key, 6), axis_at), (shards_of,), jnp.float32, least / len(cuts), high / len(cuts))
        gain = gain * jnp.repeat(jnp.exp(draws), shape[axis_at] // shards_of).reshape((-1,) + (1,) * (len(shape) - 1 - axis_at))
    return gain


def bell_draw(own_key, dims, deviation, most, shards=(), held_as=jnp.bfloat16):
    entries = deviation * jax.random.normal(own_key, dims, jnp.float32)
    if shards:
        entries = entries * level_of(own_key, dims, shards, -0.22, 0.18)
    return jnp.clip(entries, -most, most).astype(held_as)


def setup_inputs(seed: int = 0) -> dict:
    arg_keys = jax.random.split(jax.random.key(seed), 4)
    return {
        "left_blocks": bell_draw(arg_keys[0], (ROW_TILES, K_PARTS, PIECES, SA, BS, BS), 0.15, 1.2, ((0, 4), (1, 2), (2, 4)), jnp.float32),
        "right_blocks": bell_draw(arg_keys[1], (K_PARTS, PIECES, COL_TILES, SB, BS, BS), 0.15, 1.2, ((0, 2), (1, 4), (2, 4)), jnp.float32),
        "pair_stacks": draw_pair_stacks(jax.random.fold_in(arg_keys[3], 71), 0),
    }


def reference(left_blocks, right_blocks, pair_stacks):
    layer_ids = jnp.arange(K_PARTS).astype(jnp.int32)[:, None, None]
    piece_ids = jnp.arange(PIECES).astype(jnp.int32)[None, :, None]

    def tile_sum(tile_index):
        row_index = tile_index // COL_TILES
        col_index = tile_index % COL_TILES
        stacks = pair_stacks[row_index, col_index]
        left_tile = left_blocks[row_index]
        right_tile = right_blocks[:, :, col_index]
        left_slot = stacks[:, :, 0, :]
        right_slot = stacks[:, :, 1, :]
        out_slot = stacks[:, :, 2, :]
        first_blocks = left_tile[layer_ids, piece_ids, left_slot]
        second_blocks = right_tile[layer_ids, piece_ids, right_slot]
        products = jnp.einsum("lpqxy,lpqyz->lpqxz", first_blocks, second_blocks,
                              precision=lax.Precision.HIGHEST)
        summed = jax.ops.segment_sum(products.reshape(-1, BS, BS), out_slot.reshape(-1),
                                     num_segments=OUT_TILE + 1)
        return summed[:OUT_TILE]

    tiles = lax.map(tile_sum, jnp.arange(ROW_TILES * COL_TILES).astype(jnp.int32))
    return tiles.reshape(ROW_TILES, COL_TILES, OUT_TILE, BS, BS)
```

```python
import functools

import jax
import jax.numpy as jnp
from jax import lax
from jax.experimental import pallas as pl
from jax.experimental.pallas import tpu as pltpu
from jax.sharding import PartitionSpec as P

OUT_TILE = 32
GROUPS = (24, 16, 16, 8)
AHEAD = 3
FIRST = 2
EARLY = 2
LEAD = 2
MESH = pl.DeviceIdType.MESH


def kernel(
    rows, cols, left_ref, right_ref, stacks_ref, out_ref,
    left_in, right_in, left_all, slabs, twin_slab, lists, order_v, tab_v, tab_s,
    wide, pairs_a, pairs_b, buf_a, buf_b, mine_out, theirs,
    z_send, z_recv, tw_send, ex_send, ex_recv, ly_send, ly_recv, lc_send, lc_recv,
    st_send, st_recv, tab_sem, own_sem,
):
    held, sa, bs, _ = left_ref.shape
    sb = right_ref.shape[0]
    _, pieces, cap = stacks_ref.shape
    outs = out_ref.shape[0]
    half = bs // 2
    starts = tuple(sum(GROUPS[:g]) for g in range(len(GROUPS)))
    last = len(GROUPS) - 1
    zero_at = pieces * cap
    blocks = held * sa
    terms, bufs = (pairs_a, pairs_b), (buf_a, buf_b)

    row = lax.axis_index("row")
    col = lax.axis_index("col")
    layer = lax.axis_index("layer")
    other = 1 - layer
    chips = cols // 2
    sibling = col + 1 - 2 * lax.rem(col, 2)
    twin_id = {"row": row, "col": col, "layer": other}
    sibling_id = {"row": row, "col": sibling, "layer": layer}

    def row_id(at):
        return {"row": at, "col": col, "layer": layer}

    def peer_col(step):
        return lax.rem(col + 2 * step, cols)

    def peer_id(step):
        return {"row": row, "col": peer_col(step), "layer": layer}

    moves = (1, -1)
    reach = [(row + m < rows) if m > 0 else (row + m >= 0) for m in moves]
    aim = [jnp.clip(row + m, 0, rows - 1) for m in moves]

    barrier = pltpu.get_barrier_semaphore()
    greeted = jnp.int32(0)
    for may, at in zip(reach, aim):
        @pl.when(may)
        def _(at=at):
            pl.semaphore_signal(barrier, inc=1, device_id=row_id(at), device_id_type=MESH)

        greeted = greeted + may.astype(jnp.int32)

    for target in (twin_id, sibling_id) + tuple(peer_id(j) for j in range(1, chips)):
        pl.semaphore_signal(barrier, inc=1, device_id=target, device_id_type=MESH)

    own_copies = [
        pltpu.make_async_copy(right_ref, right_in, own_sem.at[0]),
        pltpu.make_async_copy(left_ref, left_in, own_sem.at[1]),
        pltpu.make_async_copy(stacks_ref, lists.at[layer], own_sem.at[2]),
    ]
    for copy in own_copies:
        copy.start()

    def piece(i):
        below, above = row, rows - 1 - row
        near = jnp.minimum(below, above)
        mixed, upward = i <= 2 * near, above > below
        step = jnp.where(mixed, lax.div(i + 1, 2), i - near)
        up = upward ^ (mixed & (lax.rem(i, 2) == 0))
        return jnp.where(up, row + step, row - step)

    def table(t):
        h = (layer, other)[t]

        def sort_rows(i, carry):
            k = piece(i)
            order_v[t, 0, pl.ds(i, 1), :cap] = lists[h, 2, pl.ds(k, 1)]
            order_v[t, 1, pl.ds(i, 1), :cap] = lists[h, 0, pl.ds(k, 1)] * sb + lists[h, 1, pl.ds(k, 1)]
            return carry

        lax.fori_loop(0, rows, sort_rows, 0)
        out_at = order_v[t, 0, :, :cap]
        place = (lax.broadcasted_iota(jnp.int32, out_at.shape, 0) * cap
                 + lax.broadcasted_iota(jnp.int32, out_at.shape, 1))
        lane = lax.broadcasted_iota(jnp.int32, (1, bs), 1)

        def link(i, carry):
            before, final = carry
            line = order_v[t, 0, pl.ds(i, 1), :cap]
            for q in range(cap):
                mine, spot = line[:, q:q + 1], i * cap + q
                before = jnp.where((out_at == mine) & (place > spot), spot, before)
                final = jnp.where(lane == mine, spot, final)
            return before, final

        before, final = lax.fori_loop(
            0, rows, link,
            (jnp.full(out_at.shape, zero_at, jnp.int32), jnp.full((1, bs), zero_at, jnp.int32)))
        tab_v[t, 0, :, :cap] = order_v[t, 1, :, :cap]
        tab_v[t, 1, :, :cap] = before
        tab_v[t, 2, 0:1] = final
        tab_copy(t).start()

    def tab_copy(t):
        return pltpu.make_async_copy(tab_v.at[t], tab_s.at[t], tab_sem.at[t])

    own_copies[0].wait()
    for b in range(sb):
        turned = right_in[b].T
        low, high = turned[:half], turned[half:]
        keep = jnp.where(layer == 0, low, high)
        give = jnp.where(layer == 0, high, low)
        for n, at in zip(GROUPS, starts):
            slabs[layer, row, sb * at + b * n:sb * at + (b + 1) * n] = keep[at:at + n]
            twin_slab[sb * at + b * n:sb * at + (b + 1) * n] = give[at:at + n]
    own_copies[1].wait()
    for i in range(held):
        for a in range(sa):
            left_all[layer, col * held + i, a] = left_in[i, a].T
    for buf in bufs:
        buf[zero_at] = jnp.zeros_like(buf[zero_at])

    own_copies[2].wait()
    table(0)
    pl.semaphore_wait(barrier, greeted + 1 + chips)

    def remote(src, dst, send, recv, target):
        return pltpu.make_async_remote_copy(
            src_ref=src, dst_ref=dst, send_sem=send, recv_sem=recv,
            device_id=target, device_id_type=MESH)

    def slab(h, k, g):
        return slabs.at[h, k, pl.ds(sb * starts[g], sb * GROUPS[g])]

    def z_copy(way, g, h, k):
        return remote(slab(h, k, g), slab(h, k, g), z_send.at[way, g, h, k], z_recv.at[g, h, k],
                      row_id(aim[way]))

    def sends(way, k):
        return reach[way] & ((k <= row) if moves[way] > 0 else (k >= row))

    def z_forward(g, h, k):
        for way in range(len(moves)):
            @pl.when(sends(way, k))
            def _(way=way):
                z_copy(way, g, h, k).start()

    def z_spread(g, h):
        z_forward(g, h, row)

    def twin_spread(g):
        z_copy(0, g, other, row).wait_recv()
        z_spread(g, other)

    def twin_part(g):
        return remote(twin_slab.at[pl.ds(sb * starts[g], sb * GROUPS[g])], slab(layer, row, g),
                      tw_send.at[g], z_recv.at[g, layer, row], twin_id)

    stack_copy = remote(stacks_ref, lists.at[layer], st_send, st_recv, twin_id)

    def left_slot(h, source, i):
        return left_all.at[h, source * held + i // sa, i % sa]

    def twin_copy(i):
        slot = left_slot(layer, col, i)
        return remote(slot, slot, ly_send.at[i], ly_recv.at[i], twin_id)

    def twin_arrival(i):
        slot = left_slot(other, col, i)
        return remote(slot, slot, ly_send.at[i], ly_recv.at[i], twin_id)

    def left_copy(kind, i, slot):
        source, target = col, sibling_id
        if slot >= chips:
            source = peer_col(cols - slot + chips - 1)
        elif slot:
            target = peer_id(slot)
        at = left_slot(layer if kind == 0 else other, source, i)
        return remote(at, at, lc_send.at[kind, i, slot], lc_recv.at[kind, i, slot], target)

    def left_arrival(kind, i, slot):
        source = sibling
        if slot >= chips:
            source = lax.rem(sibling + 2 * (cols - slot + chips - 1), cols)
        elif slot:
            source = peer_col(cols - slot)
        at = left_slot(layer if kind == 0 else other, source, i)
        return remote(at, at, lc_send.at[kind, i, slot], lc_recv.at[kind, i, slot], sibling_id)

    def relay(kind):
        for i in range(blocks):
            for j in range(1, chips):
                left_arrival(kind, i, j).wait_recv()
                left_copy(kind, i, chips - 1 + j).start()

    for g in range(AHEAD + 1):
        z_spread(g, layer)
    for g in range(FIRST):
        twin_part(g).start()
    stack_copy.start()
    for i in range(blocks):
        twin_copy(i).start()
        for slot in range(chips - 1, -1, -1):
            left_copy(0, i, slot).start()
    for g in range(FIRST, last + 1):
        twin_part(g).start()

    def pass_on(g, i, twin):
        h = (layer, other)[twin]
        k = piece(i)

        @pl.when((i > 0) & (i < rows))
        def _():
            z_copy(0, g, h, k).wait_recv()
            z_forward(g, h, k)

    def split(value):
        high = value.astype(jnp.bfloat16)
        return high, (value - high.astype(jnp.float32)).astype(jnp.bfloat16)

    def widen(h, k):
        for a in range(sa):
            high, rest = split(left_all[h, k, a])
            wide[h, k, :bs, a * bs:(a + 1) * bs] = high
            wide[h, k, bs:, a * bs:(a + 1) * bs] = rest

    def work(g, i):
        n = GROUPS[g]
        k = piece(i)
        for h, pairs in zip((layer, other), terms):
            if g == 0:
                widen(h, k)
            high, rest = split(slabs[h, k, sb * starts[g]:sb * (starts[g] + n)])
            deep = jnp.concatenate([
                jnp.concatenate([high, high], axis=1), jnp.concatenate([rest, rest], axis=1)], axis=0)
            for a in range(0, sa, 2):
                product = jnp.dot(
                    deep, wide[h, k, :, a * bs:(a + 2) * bs], preferred_element_type=jnp.float32)
                total = product[:sb * n] + product[sb * n:]
                for m in range(2):
                    pairs[(a + m) * sb:(a + m + 1) * sb, :n] = (
                        total[:, m * bs:(m + 1) * bs].reshape(sb, n, bs))

        def chain(q, carry):
            for t, (pairs, buf) in enumerate(zip(terms, bufs)):
                buf[i * cap + q, :n] = pairs[tab_s[t, 0, i, q], :n] + buf[tab_s[t, 1, i, q], :n]
            return carry

        lax.fori_loop(0, cap, chain, 0, unroll=16)

    def summed(o, n):
        return buf_a[tab_s[0, 2, 0, o], :n] + buf_b[tab_s[1, 2, 0, o], :n]

    def exchange(g):
        rng = pl.ds(starts[g], GROUPS[g])
        return remote(theirs.at[:, rng], mine_out.at[:, layer, rng], ex_send.at[g], ex_recv.at[g], twin_id)

    def exchanged(g):
        rng = pl.ds(starts[g], GROUPS[g])
        return remote(theirs.at[:, rng], mine_out.at[:, other, rng], ex_send.at[g], ex_recv.at[g], twin_id)

    def finish(g):
        n, at = GROUPS[g], starts[g]

        def give(o, carry):
            theirs[o, at:at + n] = summed(other * outs + o, n)
            return carry

        lax.fori_loop(0, outs, give, 0, unroll=8)
        exchange(g).start()

        def keep(o, carry):
            mine_out[o, layer, at:at + n] = summed(layer * outs + o, n)
            return carry

        lax.fori_loop(0, outs, keep, 0, unroll=8)

    def run(first, end, passed=None, worked=None):
        later = int(worked is not None and passed != worked)

        def step(i, carry):
            if passed is not None:
                for twin in range(2):
                    pass_on(passed, i + later, twin)
            if worked is not None:
                work(worked, i)
            return carry

        lax.fori_loop(first, end, step, 0)

    def open_group(g):
        z_spread(g, layer)
        twin_spread(g)

    at_end = (row == 0) | (row == rows - 1)
    inside = jnp.logical_not(at_end)
    for g in range(EARLY):
        twin_spread(g)

    @pl.when(inside)
    def _():
        run(1, rows // 2 + 1, passed=0)

    relay(0)
    for i in range(blocks):
        twin_arrival(i).wait_recv()
        for slot in range(chips - 1, -1, -1):
            left_copy(1, i, slot).start()
    for g in range(EARLY, AHEAD + 1):
        twin_spread(g)

    @pl.when(inside)
    def _():
        run(rows // 2 + 1, rows, passed=0)

    remote(stacks_ref, lists.at[other], st_send, st_recv, twin_id).wait_recv()
    table(1)
    relay(1)
    for kind in range(2):
        for i in range(blocks):
            for slot in (0,) + tuple(range(chips, cols - 1)):
                left_arrival(kind, i, slot).wait_recv()
    for t in range(2):
        tab_copy(t).wait()

    @pl.when(at_end)
    def _():
        for g in range(last + 1):
            if g and g + AHEAD <= last:
                open_group(g + AHEAD)
            run(0, rows, passed=g, worked=g)
            finish(g)

    @pl.when(inside)
    def _():
        for g in range(1, LEAD):
            if g + AHEAD <= last:
                open_group(g + AHEAD)
            run(1, rows, passed=g)
        for g in range(last + 1):
            ahead = g + LEAD
            if ahead + AHEAD <= last:
                open_group(ahead + AHEAD)
            run(0, rows, passed=ahead if ahead <= last else None, worked=g)
            finish(g)

    def drain(s, carry):
        h, k = lax.rem(s, 2), lax.div(s, 2)

        for way in range(len(moves)):
            @pl.when(sends(way, k))
            def _(way=way):
                for g in range(last + 1):
                    z_copy(way, g, h, k).wait_send()

        return carry

    lax.fori_loop(0, 2 * rows, drain, 0)
    stack_copy.wait_send()
    for i in range(blocks):
        twin_copy(i).wait_send()
        for kind in range(2):
            for slot in range(cols - 1):
                left_copy(kind, i, slot).wait_send()
    for g in range(last + 1):
        twin_part(g).wait_send()
        exchange(g).wait_send()
    for g in range(last + 1):
        exchanged(g).wait_recv()
    for o in range(outs):
        out_ref[o] = mine_out[o].reshape(bs, bs).T


def body(rows, cols, left_blocks, right_blocks, pair_stacks):
    left_local = left_blocks[0, 0]
    right_local = right_blocks[0, 0, 0]
    stacks = jnp.swapaxes(pair_stacks[0, 0, 0], 0, 1)
    held, sa, bs, _ = left_local.shape
    sb = right_local.shape[0]
    _, pieces, cap = stacks.shape
    outs = OUT_TILE // 2
    parts = len(GROUPS)
    tall = max(GROUPS)
    half = bs // 2
    f32 = jnp.float32
    dma = pltpu.SemaphoreType.DMA
    vmem = pl.BlockSpec(memory_space=pltpu.VMEM)
    places = pieces * cap + 1
    scratch = [
        ((held, sa, bs, bs), f32),
        ((sb, bs, bs), f32),
        ((2, pieces, sa, bs, bs), f32),
        ((2, pieces, sb * half, bs), f32),
        ((sb * half, bs), f32),
        ((2, 3, pieces, cap), jnp.int32),
        ((2, 2, pieces, bs), jnp.int32),
        ((2, 3, pieces, bs), jnp.int32),
        ((2, pieces, 2 * bs, sa * bs), jnp.bfloat16),
        ((sa * sb, tall, bs), f32),
        ((sa * sb, tall, bs), f32),
        ((places, tall, bs), f32),
        ((places, tall, bs), f32),
        ((outs, 2, half, bs), f32),
        ((outs, half, bs), f32),
    ]
    size = outs * bs * bs * 4
    for shape, kind in scratch:
        count = 1
        for d in shape:
            count *= d
        size += count * jnp.dtype(kind).itemsize
    refs = [pltpu.VMEM(shape, kind) for shape, kind in scratch]
    refs.insert(8, pltpu.SMEM((2, 3, pieces, bs), jnp.int32))
    result = pl.pallas_call(
        functools.partial(kernel, rows, cols),
        out_shape=jax.ShapeDtypeStruct((outs, bs, bs), f32),
        in_specs=[pl.BlockSpec(memory_space=pltpu.HBM)] * 3,
        out_specs=vmem,
        scratch_shapes=refs + [
            dma((2, parts, 2, pieces)),
            dma((parts, 2, pieces)),
            dma((parts,)),
            dma((parts,)),
            dma((parts,)),
            dma((held * sa,)),
            dma((held * sa,)),
            dma((2, held * sa, cols - 1)),
            dma((2, held * sa, cols - 1)),
            dma, dma,
            dma((2,)),
            dma((3,)),
        ],
        compiler_params=pltpu.CompilerParams(
            collective_id=0, has_side_effects=True, vmem_limit_bytes=size + (6 << 20)),
        name="column_window",
    )(*(pltpu.with_memory_space_constraint(v, pltpu.HBM) for v in (left_local, right_local, stacks)))
    return result[None, None]


def solution(mesh):
    placed = (
        P("row", "layer", "col", None, None, None),
        P("layer", "row", "col", None, None, None),
        P("row", "col", "layer", None, None, None),
    )
    return jax.shard_map(
        functools.partial(body, mesh.shape["row"], mesh.shape["col"]),
        mesh=mesh,
        in_specs=placed,
        out_specs=P("row", "col", "layer", None, None),
        check_vma=False,
    )
```

```python
import functools

import jax
import jax.numpy as jnp
from jax import lax
from jax.experimental import pallas as pl
from jax.experimental.pallas import tpu as pltpu
from jax.sharding import PartitionSpec as P

OUT_TILE = 32
GROUPS = (24, 16, 16, 8)
AHEAD = 3
FIRST = 2
EARLY = 2
LEAD = 2
MESH = pl.DeviceIdType.MESH


def kernel(
    rows, cols, left_ref, right_ref, stacks_ref, out_ref,
    left_in, right_in, left_all, slabs, twin_slab, lists, order_v, tab_v, tab_s,
    wide, pairs_a, pairs_b, buf_a, buf_b, mine_out, theirs,
    z_send, z_recv, tw_send, ex_send, ex_recv, ly_send, ly_recv, lc_send, lc_recv,
    st_send, st_recv, tab_sem, own_sem,
):
    held, sa, bs, _ = left_ref.shape
    sb = right_ref.shape[0]
    _, pieces, cap = stacks_ref.shape
    outs = out_ref.shape[0]
    half = bs // 2
    starts = tuple(sum(GROUPS[:g]) for g in range(len(GROUPS)))
    last = len(GROUPS) - 1
    zero_at = pieces * cap
    blocks = held * sa
    terms, bufs = (pairs_a, pairs_b), (buf_a, buf_b)

    row = lax.axis_index("row")
    col = lax.axis_index("col")
    layer = lax.axis_index("layer")
    other = 1 - layer
    chips = cols // 2
    sibling = col + 1 - 2 * lax.rem(col, 2)
    twin_id = {"row": row, "col": col, "layer": other}
    sibling_id = {"row": row, "col": sibling, "layer": layer}

    def row_id(at):
        return {"row": at, "col": col, "layer": layer}

    def peer_col(step):
        return lax.rem(col + 2 * step, cols)

    def peer_id(step):
        return {"row": row, "col": peer_col(step), "layer": layer}

    moves = (1, -1)
    reach = [(row + m < rows) if m > 0 else (row + m >= 0) for m in moves]
    aim = [jnp.clip(row + m, 0, rows - 1) for m in moves]

    barrier = pltpu.get_barrier_semaphore()
    greeted = jnp.int32(0)
    for may, at in zip(reach, aim):
        @pl.when(may)
        def _(at=at):
            pl.semaphore_signal(barrier, inc=1, device_id=row_id(at), device_id_type=MESH)

        greeted = greeted + may.astype(jnp.int32)

    for target in (twin_id, sibling_id) + tuple(peer_id(j) for j in range(1, chips)):
        pl.semaphore_signal(barrier, inc=1, device_id=target, device_id_type=MESH)

    own_copies = [
        pltpu.make_async_copy(right_ref, right_in, own_sem.at[0]),
        pltpu.make_async_copy(left_ref, left_in, own_sem.at[1]),
        pltpu.make_async_copy(stacks_ref, lists.at[layer], own_sem.at[2]),
    ]
    for copy in own_copies:
        copy.start()

    def piece(i):
        below, above = row, rows - 1 - row
        near = jnp.minimum(below, above)
        mixed, upward = i <= 2 * near, above > below
        step = jnp.where(mixed, lax.div(i + 1, 2), i - near)
        up = upward ^ (mixed & (lax.rem(i, 2) == 0))
        return jnp.where(up, row + step, row - step)

    def table(t):
        h = (layer, other)[t]

        def sort_rows(i, carry):
            k = piece(i)
            order_v[t, 0, pl.ds(i, 1), :cap] = lists[h, 2, pl.ds(k, 1)]
            order_v[t, 1, pl.ds(i, 1), :cap] = lists[h, 0, pl.ds(k, 1)] * sb + lists[h, 1, pl.ds(k, 1)]
            return carry

        lax.fori_loop(0, rows, sort_rows, 0)
        out_at = order_v[t, 0, :, :cap]
        place = (lax.broadcasted_iota(jnp.int32, out_at.shape, 0) * cap
                 + lax.broadcasted_iota(jnp.int32, out_at.shape, 1))
        lane = lax.broadcasted_iota(jnp.int32, (1, bs), 1)

        def link(i, carry):
            before, final = carry
            line = order_v[t, 0, pl.ds(i, 1), :cap]
            for q in range(cap):
                mine, spot = line[:, q:q + 1], i * cap + q
                before = jnp.where((out_at == mine) & (place > spot), spot, before)
                final = jnp.where(lane == mine, spot, final)
            return before, final

        before, final = lax.fori_loop(
            0, rows, link,
            (jnp.full(out_at.shape, zero_at, jnp.int32), jnp.full((1, bs), zero_at, jnp.int32)))
        tab_v[t, 0, :, :cap] = order_v[t, 1, :, :cap]
        tab_v[t, 1, :, :cap] = before
        tab_v[t, 2, 0:1] = final
        tab_copy(t).start()

    def tab_copy(t):
        return pltpu.make_async_copy(tab_v.at[t], tab_s.at[t], tab_sem.at[t])

    own_copies[0].wait()
    for b in range(sb):
        turned = right_in[b].T
        low, high = turned[:half], turned[half:]
        keep = jnp.where(layer == 0, low, high)
        give = jnp.where(layer == 0, high, low)
        for n, at in zip(GROUPS, starts):
            slabs[layer, row, sb * at + b * n:sb * at + (b + 1) * n] = keep[at:at + n]
            twin_slab[sb * at + b * n:sb * at + (b + 1) * n] = give[at:at + n]
    own_copies[1].wait()
    for i in range(held):
        for a in range(sa):
            left_all[layer, col * held + i, a] = left_in[i, a].T
    for buf in bufs:
        buf[zero_at] = jnp.zeros_like(buf[zero_at])

    own_copies[2].wait()
    pl.semaphore_wait(barrier, greeted + 1 + chips)

    def remote(src, dst, send, recv, target):
        return pltpu.make_async_remote_copy(
            src_ref=src, dst_ref=dst, send_sem=send, recv_sem=recv,
            device_id=target, device_id_type=MESH)

    def slab(h, k, g):
        return slabs.at[h, k, pl.ds(sb * starts[g], sb * GROUPS[g])]

    def z_copy(way, g, h, k):
        return remote(slab(h, k, g), slab(h, k, g), z_send.at[way, g, h, k], z_recv.at[g, h, k],
                      row_id(aim[way]))

    def sends(way, k):
        return reach[way] & ((k <= row) if moves[way] > 0 else (k >= row))

    def z_forward(g, h, k):
        for way in range(len(moves)):
            @pl.when(sends(way, k))
            def _(way=way):
                z_copy(way, g, h, k).start()

    def z_spread(g, h):
        z_forward(g, h, row)

    def twin_spread(g):
        z_copy(0, g, other, row).wait_recv()
        z_spread(g, other)

    def twin_part(g):
        return remote(twin_slab.at[pl.ds(sb * starts[g], sb * GROUPS[g])], slab(layer, row, g),
                      tw_send.at[g], z_recv.at[g, layer, row], twin_id)

    stack_copy = remote(stacks_ref, lists.at[layer], st_send, st_recv, twin_id)

    def left_slot(h, source, i):
        return left_all.at[h, source * held + i // sa, i % sa]

    def twin_copy(i):
        slot = left_slot(layer, col, i)
        return remote(slot, slot, ly_send.at[i], ly_recv.at[i], twin_id)

    def twin_arrival(i):
        slot = left_slot(other, col, i)
        return remote(slot, slot, ly_send.at[i], ly_recv.at[i], twin_id)

    def left_copy(kind, i, slot):
        source, target = col, sibling_id
        if slot >= chips:
            source = peer_col(cols - slot + chips - 1)
        elif slot:
            target = peer_id(slot)
        at = left_slot(layer if kind == 0 else other, source, i)
        return remote(at, at, lc_send.at[kind, i, slot], lc_recv.at[kind, i, slot], target)

    def left_arrival(kind, i, slot):
        source = sibling
        if slot >= chips:
            source = lax.rem(sibling + 2 * (cols - slot + chips - 1), cols)
        elif slot:
            source = peer_col(cols - slot)
        at = left_slot(layer if kind == 0 else other, source, i)
        return remote(at, at, lc_send.at[kind, i, slot], lc_recv.at[kind, i, slot], sibling_id)

    def relay(kind):
        for i in range(blocks):
            for j in range(1, chips):
                left_arrival(kind, i, j).wait_recv()
                left_copy(kind, i, chips - 1 + j).start()

    z_spread(0, layer)
    stack_copy.start()
    for g in range(FIRST):
        twin_part(g).start()
    for i in range(blocks):
        twin_copy(i).start()
        for slot in range(chips - 1, -1, -1):
            left_copy(0, i, slot).start()
    for g in range(1, AHEAD + 1):
        z_spread(g, layer)
    for g in range(FIRST, last + 1):
        twin_part(g).start()

    def pass_on(g, i, twin):
        h = (layer, other)[twin]
        k = piece(i)

        @pl.when((i > 0) & (i < rows))
        def _():
            z_copy(0, g, h, k).wait_recv()
            z_forward(g, h, k)

    def split(value):
        high = value.astype(jnp.bfloat16)
        return high, (value - high.astype(jnp.float32)).astype(jnp.bfloat16)

    def widen(h, k):
        for a in range(sa):
            high, rest = split(left_all[h, k, a])
            wide[h, k, :bs, a * bs:(a + 1) * bs] = high
            wide[h, k, bs:, a * bs:(a + 1) * bs] = rest

    def work(g, i):
        n = GROUPS[g]
        k = piece(i)
        for h, pairs in zip((layer, other), terms):
            if g == 0:
                widen(h, k)
            high, rest = split(slabs[h, k, sb * starts[g]:sb * (starts[g] + n)])
            deep = jnp.concatenate([
                jnp.concatenate([high, high], axis=1), jnp.concatenate([rest, rest], axis=1)], axis=0)
            for a in range(0, sa, 2):
                product = jnp.dot(
                    deep, wide[h, k, :, a * bs:(a + 2) * bs], preferred_element_type=jnp.float32)
                total = product[:sb * n] + product[sb * n:]
                for m in range(2):
                    pairs[(a + m) * sb:(a + m + 1) * sb, :n] = (
                        total[:, m * bs:(m + 1) * bs].reshape(sb, n, bs))

        def chain(q, carry):
            for t, (pairs, buf) in enumerate(zip(terms, bufs)):
                buf[i * cap + q, :n] = pairs[tab_s[t, 0, i, q], :n] + buf[tab_s[t, 1, i, q], :n]
            return carry

        lax.fori_loop(0, cap, chain, 0, unroll=16)

    def summed(o, n):
        return buf_a[tab_s[0, 2, 0, o], :n] + buf_b[tab_s[1, 2, 0, o], :n]

    def exchange(g):
        rng = pl.ds(outs * starts[g], outs * GROUPS[g])
        return remote(theirs.at[rng], mine_out.at[layer, rng], ex_send.at[g], ex_recv.at[g], twin_id)

    def exchanged(g):
        rng = pl.ds(outs * starts[g], outs * GROUPS[g])
        return remote(theirs.at[rng], mine_out.at[other, rng], ex_send.at[g], ex_recv.at[g], twin_id)

    def finish(g):
        n, at = GROUPS[g], outs * starts[g]

        def give(o, carry):
            theirs[pl.ds(pl.multiple_of(at + o * n, 8), n)] = summed(other * outs + o, n)
            return carry

        lax.fori_loop(0, outs, give, 0, unroll=8)
        exchange(g).start()

        def keep(o, carry):
            mine_out[layer, pl.ds(pl.multiple_of(at + o * n, 8), n)] = summed(layer * outs + o, n)
            return carry

        lax.fori_loop(0, outs, keep, 0, unroll=8)

    def run(first, end, passed=None, worked=None):
        later = int(worked is not None and passed != worked)

        def step(i, carry):
            if passed is not None:
                for twin in range(2):
                    pass_on(passed, i + later, twin)
            if worked is not None:
                work(worked, i)
            return carry

        lax.fori_loop(first, end, step, 0)

    def open_group(g):
        z_spread(g, layer)
        twin_spread(g)

    at_end = (row == 0) | (row == rows - 1)
    inside = jnp.logical_not(at_end)
    table(0)
    remote(stacks_ref, lists.at[other], st_send, st_recv, twin_id).wait_recv()
    table(1)
    for g in range(EARLY):
        twin_spread(g)

    @pl.when(inside)
    def _():
        run(1, rows // 2 + 1, passed=0)

    relay(0)
    for i in range(blocks):
        twin_arrival(i).wait_recv()
        for slot in range(chips - 1, -1, -1):
            left_copy(1, i, slot).start()
    for g in range(EARLY, AHEAD + 1):
        twin_spread(g)

    @pl.when(inside)
    def _():
        run(rows // 2 + 1, rows, passed=0)

    relay(1)

    @pl.when(inside)
    def _():
        for g in range(1, LEAD):
            run(1, rows, passed=g)

    for kind in range(2):
        for i in range(blocks):
            for slot in (0,) + tuple(range(chips, cols - 1)):
                left_arrival(kind, i, slot).wait_recv()
    for t in range(2):
        tab_copy(t).wait()

    @pl.when(at_end)
    def _():
        for g in range(last + 1):
            if g and g + AHEAD <= last:
                open_group(g + AHEAD)
            run(0, rows, passed=g, worked=g)
            finish(g)

    @pl.when(inside)
    def _():
        for g in range(last + 1):
            ahead = g + LEAD
            if ahead + AHEAD <= last:
                open_group(ahead + AHEAD)
            run(0, rows, passed=ahead if ahead <= last else None, worked=g)
            finish(g)

    def drain(s, carry):
        h, k = lax.rem(s, 2), lax.div(s, 2)

        for way in range(len(moves)):
            @pl.when(sends(way, k))
            def _(way=way):
                for g in range(last + 1):
                    z_copy(way, g, h, k).wait_send()

        return carry

    lax.fori_loop(0, 2 * rows, drain, 0)
    stack_copy.wait_send()
    for i in range(blocks):
        twin_copy(i).wait_send()
        for kind in range(2):
            for slot in range(cols - 1):
                left_copy(kind, i, slot).wait_send()
    for g in range(last + 1):
        twin_part(g).wait_send()
        exchange(g).wait_send()
    for g in range(last + 1):
        exchanged(g).wait_recv()
    for o in range(outs):
        out_ref[o] = jnp.concatenate([
            mine_out[side, outs * at + o * n:outs * at + (o + 1) * n]
            for side in range(2) for n, at in zip(GROUPS, starts)], axis=0).T


def body(rows, cols, left_blocks, right_blocks, pair_stacks):
    left_local = left_blocks[0, 0]
    right_local = right_blocks[0, 0, 0]
    stacks = jnp.swapaxes(pair_stacks[0, 0, 0], 0, 1)
    held, sa, bs, _ = left_local.shape
    sb = right_local.shape[0]
    _, pieces, cap = stacks.shape
    outs = OUT_TILE // 2
    parts = len(GROUPS)
    tall = max(GROUPS)
    half = bs // 2
    f32 = jnp.float32
    dma = pltpu.SemaphoreType.DMA
    vmem = pl.BlockSpec(memory_space=pltpu.VMEM)
    places = pieces * cap + 1
    scratch = [
        ((held, sa, bs, bs), f32),
        ((sb, bs, bs), f32),
        ((2, pieces, sa, bs, bs), f32),
        ((2, pieces, sb * half, bs), f32),
        ((sb * half, bs), f32),
        ((2, 3, pieces, cap), jnp.int32),
        ((2, 2, pieces, bs), jnp.int32),
        ((2, 3, pieces, bs), jnp.int32),
        ((2, pieces, 2 * bs, sa * bs), jnp.bfloat16),
        ((sa * sb, tall, bs), f32),
        ((sa * sb, tall, bs), f32),
        ((places, tall, bs), f32),
        ((places, tall, bs), f32),
        ((2, outs * half, bs), f32),
        ((outs * half, bs), f32),
    ]
    size = outs * bs * bs * 4
    for shape, kind in scratch:
        count = 1
        for d in shape:
            count *= d
        size += count * jnp.dtype(kind).itemsize
    refs = [pltpu.VMEM(shape, kind) for shape, kind in scratch]
    refs.insert(8, pltpu.SMEM((2, 3, pieces, bs), jnp.int32))
    result = pl.pallas_call(
        functools.partial(kernel, rows, cols),
        out_shape=jax.ShapeDtypeStruct((outs, bs, bs), f32),
        in_specs=[pl.BlockSpec(memory_space=pltpu.HBM)] * 3,
        out_specs=vmem,
        scratch_shapes=refs + [
            dma((2, parts, 2, pieces)),
            dma((parts, 2, pieces)),
            dma((parts,)),
            dma((parts,)),
            dma((parts,)),
            dma((held * sa,)),
            dma((held * sa,)),
            dma((2, held * sa, cols - 1)),
            dma((2, held * sa, cols - 1)),
            dma, dma,
            dma((2,)),
            dma((3,)),
        ],
        compiler_params=pltpu.CompilerParams(
            collective_id=0, has_side_effects=True, vmem_limit_bytes=size + (6 << 20)),
        name="column_window",
    )(*(pltpu.with_memory_space_constraint(v, pltpu.HBM) for v in (left_local, right_local, stacks)))
    return result[None, None]


def solution(mesh):
    placed = (
        P("row", "layer", "col", None, None, None),
        P("layer", "row", "col", None, None, None),
        P("row", "col", "layer", None, None, None),
    )
    return jax.shard_map(
        functools.partial(body, mesh.shape["row"], mesh.shape["col"]),
        mesh=mesh,
        in_specs=placed,
        out_specs=P("row", "col", "layer", None, None),
        check_vma=False,
    )
```

```python
import functools

import jax
import jax.numpy as jnp
from jax import lax
from jax.experimental import pallas as pl
from jax.experimental.pallas import tpu as pltpu
from jax.sharding import PartitionSpec as P

OUT_TILE = 32
GROUPS = (24, 16, 16, 8)
AHEAD = 3
FIRST = 2
EARLY = 2
LEAD = 2
MESH = pl.DeviceIdType.MESH


def kernel(
    rows, cols, left_ref, right_ref, stacks_ref, out_ref,
    left_in, right_in, left_all, slabs, twin_slab, lists, order_v, tab_v, tab_s,
    wide, pairs_a, pairs_b, buf_a, buf_b, theirs,
    z_send, z_recv, tw_send, ex_send, ex_recv, ly_send, ly_recv, lc_send, lc_recv,
    st_send, st_recv, tab_sem, own_sem,
):
    held, sa, bs, _ = left_ref.shape
    sb = right_ref.shape[0]
    _, pieces, cap = stacks_ref.shape
    outs = OUT_TILE // 2
    mine_out = out_ref
    half = bs // 2
    starts = tuple(sum(GROUPS[:g]) for g in range(len(GROUPS)))
    last = len(GROUPS) - 1
    zero_at = pieces * cap
    blocks = held * sa
    terms, bufs = (pairs_a, pairs_b), (buf_a, buf_b)

    row = lax.axis_index("row")
    col = lax.axis_index("col")
    layer = lax.axis_index("layer")
    other = 1 - layer
    chips = cols // 2
    sibling = col + 1 - 2 * lax.rem(col, 2)
    twin_id = {"row": row, "col": col, "layer": other}
    sibling_id = {"row": row, "col": sibling, "layer": layer}

    def row_id(at):
        return {"row": at, "col": col, "layer": layer}

    def peer_col(step):
        return lax.rem(col + 2 * step, cols)

    def peer_id(step):
        return {"row": row, "col": peer_col(step), "layer": layer}

    moves = (1, -1)
    reach = [(row + m < rows) if m > 0 else (row + m >= 0) for m in moves]
    aim = [jnp.clip(row + m, 0, rows - 1) for m in moves]

    barrier = pltpu.get_barrier_semaphore()
    greeted = jnp.int32(0)
    for may, at in zip(reach, aim):
        @pl.when(may)
        def _(at=at):
            pl.semaphore_signal(barrier, inc=1, device_id=row_id(at), device_id_type=MESH)

        greeted = greeted + may.astype(jnp.int32)

    for target in (twin_id, sibling_id) + tuple(peer_id(j) for j in range(1, chips)):
        pl.semaphore_signal(barrier, inc=1, device_id=target, device_id_type=MESH)

    own_copies = [
        pltpu.make_async_copy(right_ref, right_in, own_sem.at[0]),
        pltpu.make_async_copy(left_ref, left_in, own_sem.at[1]),
        pltpu.make_async_copy(stacks_ref, lists.at[layer], own_sem.at[2]),
    ]
    for copy in own_copies:
        copy.start()

    def piece(i):
        below, above = row, rows - 1 - row
        near = jnp.minimum(below, above)
        mixed, upward = i <= 2 * near, above > below
        step = jnp.where(mixed, lax.div(i + 1, 2), i - near)
        up = upward ^ (mixed & (lax.rem(i, 2) == 0))
        return jnp.where(up, row + step, row - step)

    def table(t):
        h = jnp.where(t == 0, layer, other)

        def sort_rows(i, carry):
            k = piece(i)
            order_v[t, 0, pl.ds(i, 1), :cap] = lists[h, 2, pl.ds(k, 1)]
            order_v[t, 1, pl.ds(i, 1), :cap] = lists[h, 0, pl.ds(k, 1)] * sb + lists[h, 1, pl.ds(k, 1)]
            return carry

        lax.fori_loop(0, rows, sort_rows, 0)
        out_at = order_v[t, 0, :, :cap]
        place = (lax.broadcasted_iota(jnp.int32, out_at.shape, 0) * cap
                 + lax.broadcasted_iota(jnp.int32, out_at.shape, 1))
        lane = lax.broadcasted_iota(jnp.int32, (1, bs), 1)

        def link(i, carry):
            before, final = carry
            line = order_v[t, 0, pl.ds(i, 1), :cap]
            for q in range(cap):
                mine, spot = line[:, q:q + 1], i * cap + q
                before = jnp.where((out_at == mine) & (place > spot), spot, before)
                final = jnp.where(lane == mine, spot, final)
            return before, final

        before, final = lax.fori_loop(
            0, rows, link,
            (jnp.full(out_at.shape, zero_at, jnp.int32), jnp.full((1, bs), zero_at, jnp.int32)))
        tab_v[t, 0, :, :cap] = order_v[t, 1, :, :cap]
        tab_v[t, 1, :, :cap] = before
        tab_v[t, 2, 0:1] = final
        tab_copy(t).start()

    def tab_copy(t):
        return pltpu.make_async_copy(tab_v.at[t], tab_s.at[t], tab_sem.at[t])

    own_copies[0].wait()
    for b in range(sb):
        turned = right_in[b].T
        low, high = turned[:half], turned[half:]
        keep = jnp.where(layer == 0, low, high)
        give = jnp.where(layer == 0, high, low)
        for n, at in zip(GROUPS, starts):
            slabs[layer, row, sb * at + b * n:sb * at + (b + 1) * n] = keep[at:at + n]
            twin_slab[sb * at + b * n:sb * at + (b + 1) * n] = give[at:at + n]
    own_copies[1].wait()
    for i in range(held):
        for a in range(sa):
            left_all[layer, col * held + i, a] = left_in[i, a].T
    for buf in bufs:
        buf[zero_at] = jnp.zeros_like(buf[zero_at])

    own_copies[2].wait()
    pl.semaphore_wait(barrier, greeted + 1 + chips)

    def remote(src, dst, send, recv, target):
        return pltpu.make_async_remote_copy(
            src_ref=src, dst_ref=dst, send_sem=send, recv_sem=recv,
            device_id=target, device_id_type=MESH)

    def slab(h, k, g):
        return slabs.at[h, k, pl.ds(sb * starts[g], sb * GROUPS[g])]

    def z_copy(way, g, h, k):
        return remote(slab(h, k, g), slab(h, k, g), z_send.at[way, g, h, k], z_recv.at[g, h, k],
                      row_id(aim[way]))

    def sends(way, k):
        return reach[way] & ((k <= row) if moves[way] > 0 else (k >= row))

    def z_forward(g, h, k):
        for way in range(len(moves)):
            @pl.when(sends(way, k))
            def _(way=way):
                z_copy(way, g, h, k).start()

    def z_spread(g, h):
        z_forward(g, h, row)

    def twin_spread(g):
        z_copy(0, g, other, row).wait_recv()
        z_spread(g, other)

    def twin_part(g):
        return remote(twin_slab.at[pl.ds(sb * starts[g], sb * GROUPS[g])], slab(layer, row, g),
                      tw_send.at[g], z_recv.at[g, layer, row], twin_id)

    stack_copy = remote(stacks_ref, lists.at[layer], st_send, st_recv, twin_id)

    def left_slot(h, source, i):
        return left_all.at[h, source * held + i // sa, i % sa]

    def twin_copy(i):
        slot = left_slot(layer, col, i)
        return remote(slot, slot, ly_send.at[i], ly_recv.at[i], twin_id)

    def twin_arrival(i):
        slot = left_slot(other, col, i)
        return remote(slot, slot, ly_send.at[i], ly_recv.at[i], twin_id)

    def left_copy(kind, i, slot):
        source, target = col, sibling_id
        if slot >= chips:
            source = peer_col(cols - slot + chips - 1)
        elif slot:
            target = peer_id(slot)
        at = left_slot(layer if kind == 0 else other, source, i)
        return remote(at, at, lc_send.at[kind, i, slot], lc_recv.at[kind, i, slot], target)

    def left_arrival(kind, i, slot):
        source = sibling
        if slot >= chips:
            source = lax.rem(sibling + 2 * (cols - slot + chips - 1), cols)
        elif slot:
            source = peer_col(cols - slot)
        at = left_slot(layer if kind == 0 else other, source, i)
        return remote(at, at, lc_send.at[kind, i, slot], lc_recv.at[kind, i, slot], sibling_id)

    def relay(kind):
        for i in range(blocks):
            for j in range(1, chips):
                left_arrival(kind, i, j).wait_recv()
                left_copy(kind, i, chips - 1 + j).start()

    z_spread(0, layer)
    stack_copy.start()
    for g in range(FIRST):
        twin_part(g).start()
    for i in range(blocks):
        twin_copy(i).start()
        for slot in range(chips - 1, -1, -1):
            left_copy(0, i, slot).start()
    for g in range(1, AHEAD + 1):
        z_spread(g, layer)
    for g in range(FIRST, last + 1):
        twin_part(g).start()

    def pass_on(g, i, twin):
        h = (layer, other)[twin]
        k = piece(i)

        @pl.when((i > 0) & (i < rows))
        def _():
            z_copy(0, g, h, k).wait_recv()
            z_forward(g, h, k)

    def split(value):
        high = value.astype(jnp.bfloat16)
        return high, (value - high.astype(jnp.float32)).astype(jnp.bfloat16)

    def widen(h, k):
        for a in range(sa):
            high, rest = split(left_all[h, k, a])
            wide[h, k, :bs, a * bs:(a + 1) * bs] = high
            wide[h, k, bs:, a * bs:(a + 1) * bs] = rest

    def work(g, i):
        n = GROUPS[g]
        k = piece(i)
        for h, pairs in zip((layer, other), terms):
            if g == 0:
                widen(h, k)
            high, rest = split(slabs[h, k, sb * starts[g]:sb * (starts[g] + n)])
            deep = jnp.concatenate([
                jnp.concatenate([high, high], axis=1), jnp.concatenate([rest, rest], axis=1)], axis=0)
            for a in range(0, sa, 2):
                product = jnp.dot(
                    deep, wide[h, k, :, a * bs:(a + 2) * bs], preferred_element_type=jnp.float32)
                total = product[:sb * n] + product[sb * n:]
                for m in range(2):
                    pairs[(a + m) * sb:(a + m + 1) * sb, :n] = (
                        total[:, m * bs:(m + 1) * bs].reshape(sb, n, bs))

        def chain(q, carry):
            for t, (pairs, buf) in enumerate(zip(terms, bufs)):
                buf[i * cap + q, :n] = pairs[tab_s[t, 0, i, q], :n] + buf[tab_s[t, 1, i, q], :n]
            return carry

        lax.fori_loop(0, cap, chain, 0, unroll=16)

    def summed(o, n):
        return buf_a[tab_s[0, 2, 0, o], :n] + buf_b[tab_s[1, 2, 0, o], :n]

    def exchange(g):
        rng = pl.ds(outs * starts[g], outs * GROUPS[g])
        return remote(theirs.at[rng], mine_out.at[layer, rng], ex_send.at[g], ex_recv.at[g], twin_id)

    def exchanged(g):
        rng = pl.ds(outs * starts[g], outs * GROUPS[g])
        return remote(theirs.at[rng], mine_out.at[other, rng], ex_send.at[g], ex_recv.at[g], twin_id)

    def finish(g):
        n, at = GROUPS[g], outs * starts[g]

        def give(o, carry):
            theirs[pl.ds(pl.multiple_of(at + o * n, 8), n)] = summed(other * outs + o, n)
            return carry

        lax.fori_loop(0, outs, give, 0, unroll=8)
        exchange(g).start()

        def keep(o, carry):
            mine_out[layer, pl.ds(pl.multiple_of(at + o * n, 8), n)] = summed(layer * outs + o, n)
            return carry

        lax.fori_loop(0, outs, keep, 0, unroll=8)

    def run(first, end, passed=None, worked=None):
        later = int(worked is not None and passed != worked)

        def step(i, carry):
            if passed is not None:
                for twin in range(2):
                    pass_on(passed, i + later, twin)
            if worked is not None:
                work(worked, i)
            return carry

        lax.fori_loop(first, end, step, 0)

    def open_group(g):
        z_spread(g, layer)
        twin_spread(g)

    at_end = (row == 0) | (row == rows - 1)
    inside = jnp.logical_not(at_end)
    remote(stacks_ref, lists.at[other], st_send, st_recv, twin_id).wait_recv()

    def tables(t, carry):
        table(t)
        return carry

    lax.fori_loop(0, 2, tables, 0)
    for g in range(EARLY):
        twin_spread(g)

    @pl.when(inside)
    def _():
        run(1, rows // 2 + 1, passed=0)

    relay(0)
    for i in range(blocks):
        twin_arrival(i).wait_recv()
        for slot in range(chips - 1, -1, -1):
            left_copy(1, i, slot).start()
    for g in range(EARLY, AHEAD + 1):
        twin_spread(g)

    @pl.when(inside)
    def _():
        run(rows // 2 + 1, rows, passed=0)

    relay(1)

    @pl.when(inside)
    def _():
        for g in range(1, LEAD):
            run(1, rows, passed=g)

    for kind in range(2):
        for i in range(blocks):
            for slot in (0,) + tuple(range(chips, cols - 1)):
                left_arrival(kind, i, slot).wait_recv()
    for t in range(2):
        tab_copy(t).wait()

    @pl.when(at_end)
    def _():
        for g in range(last + 1):
            if g and g + AHEAD <= last:
                open_group(g + AHEAD)
            run(0, rows, passed=g, worked=g)
            finish(g)

    @pl.when(inside)
    def _():
        for g in range(last + 1):
            ahead = g + LEAD
            if ahead + AHEAD <= last:
                open_group(ahead + AHEAD)
            run(0, rows, passed=ahead if ahead <= last else None, worked=g)
            finish(g)

    def drain(s, carry):
        h, k = lax.rem(s, 2), lax.div(s, 2)

        for way in range(len(moves)):
            @pl.when(sends(way, k))
            def _(way=way):
                for g in range(last + 1):
                    z_copy(way, g, h, k).wait_send()

        return carry

    lax.fori_loop(0, 2 * rows, drain, 0)
    stack_copy.wait_send()
    for i in range(blocks):
        twin_copy(i).wait_send()
        for kind in range(2):
            for slot in range(cols - 1):
                left_copy(kind, i, slot).wait_send()
    for g in range(last + 1):
        twin_part(g).wait_send()
        exchange(g).wait_send()
    for g in range(last + 1):
        exchanged(g).wait_recv()


def turn(parts_ref, out_ref, held, sems):
    outs = out_ref.shape[0]
    starts = tuple(sum(GROUPS[:g]) for g in range(len(GROUPS)))
    copies = []
    for o in range(outs):
        held[o] = jnp.concatenate([
            parts_ref[side, outs * at + o * n:outs * at + (o + 1) * n]
            for side in range(2) for n, at in zip(GROUPS, starts)], axis=0).T
        copies.append(pltpu.make_async_copy(held.at[o], out_ref.at[o], sems.at[o]))
        copies[-1].start()
    for copy in copies:
        copy.wait()


def body(rows, cols, left_blocks, right_blocks, pair_stacks):
    left_local = left_blocks[0, 0]
    right_local = right_blocks[0, 0, 0]
    stacks = jnp.swapaxes(pair_stacks[0, 0, 0], 0, 1)
    held, sa, bs, _ = left_local.shape
    sb = right_local.shape[0]
    _, pieces, cap = stacks.shape
    outs = OUT_TILE // 2
    parts = len(GROUPS)
    tall = max(GROUPS)
    half = bs // 2
    f32 = jnp.float32
    dma = pltpu.SemaphoreType.DMA
    vmem = pl.BlockSpec(memory_space=pltpu.VMEM)
    places = pieces * cap + 1
    scratch = [
        ((held, sa, bs, bs), f32),
        ((sb, bs, bs), f32),
        ((2, pieces, sa, bs, bs), f32),
        ((2, pieces, sb * half, bs), f32),
        ((sb * half, bs), f32),
        ((2, 3, pieces, cap), jnp.int32),
        ((2, 2, pieces, bs), jnp.int32),
        ((2, 3, pieces, bs), jnp.int32),
        ((2, pieces, 2 * bs, sa * bs), jnp.bfloat16),
        ((sa * sb, tall, bs), f32),
        ((sa * sb, tall, bs), f32),
        ((places, tall, bs), f32),
        ((places, tall, bs), f32),
        ((outs * half, bs), f32),
    ]
    size = outs * bs * bs * 4
    for shape, kind in scratch:
        count = 1
        for d in shape:
            count *= d
        size += count * jnp.dtype(kind).itemsize
    refs = [pltpu.VMEM(shape, kind) for shape, kind in scratch]
    refs.insert(8, pltpu.SMEM((2, 3, pieces, bs), jnp.int32))
    result = pl.pallas_call(
        functools.partial(kernel, rows, cols),
        out_shape=jax.ShapeDtypeStruct((2, outs * half, bs), f32),
        in_specs=[pl.BlockSpec(memory_space=pltpu.HBM)] * 3,
        out_specs=vmem,
        scratch_shapes=refs + [
            dma((2, parts, 2, pieces)),
            dma((parts, 2, pieces)),
            dma((parts,)),
            dma((parts,)),
            dma((parts,)),
            dma((held * sa,)),
            dma((held * sa,)),
            dma((2, held * sa, cols - 1)),
            dma((2, held * sa, cols - 1)),
            dma, dma,
            dma((2,)),
            dma((3,)),
        ],
        compiler_params=pltpu.CompilerParams(
            collective_id=0, has_side_effects=True, vmem_limit_bytes=size + (6 << 20)),
        name="column_window",
    )(*(pltpu.with_memory_space_constraint(v, pltpu.HBM) for v in (left_local, right_local, stacks)))
    turned = pl.pallas_call(
        turn,
        out_shape=jax.ShapeDtypeStruct((outs, bs, bs), f32),
        in_specs=[vmem],
        out_specs=pl.BlockSpec(memory_space=pltpu.HBM),
        scratch_shapes=[pltpu.VMEM((outs, bs, bs), f32), dma((outs,))],
        compiler_params=pltpu.CompilerParams(vmem_limit_bytes=8 << 20),
        name="turn",
    )(result)
    return turned[None, None]


def solution(mesh):
    placed = (
        P("row", "layer", "col", None, None, None),
        P("layer", "row", "col", None, None, None),
        P("row", "col", "layer", None, None, None),
    )
    return jax.shard_map(
        functools.partial(body, mesh.shape["row"], mesh.shape["col"]),
        mesh=mesh,
        in_specs=placed,
        out_specs=P("row", "col", "layer", None, None),
        check_vma=False,
    )
```

```python
import functools

import jax
import jax.numpy as jnp
from jax import lax
from jax.experimental import pallas as pl
from jax.experimental.pallas import tpu as pltpu
from jax.sharding import PartitionSpec as P

OUT_TILE = 32
GROUPS = (32, 16, 8, 8)
AHEAD = 3
FIRST = 2
EARLY = 2
LEAD = 2
MESH = pl.DeviceIdType.MESH


def kernel(
    rows, cols, left_ref, right_ref, stacks_ref, out_ref,
    left_in, right_in, left_all, slabs, twin_slab, lists, order_v, tab_v, tab_s,
    wide, pairs_a, pairs_b, buf_a, buf_b, theirs,
    z_send, z_recv, tw_send, ex_send, ex_recv, ly_send, ly_recv, lc_send, lc_recv,
    st_send, st_recv, tab_sem, own_sem,
):
    held, sa, bs, _ = left_ref.shape
    sb = right_ref.shape[0]
    _, pieces, cap = stacks_ref.shape
    outs = OUT_TILE // 2
    mine_out = out_ref
    half = bs // 2
    starts = tuple(sum(GROUPS[:g]) for g in range(len(GROUPS)))
    last = len(GROUPS) - 1
    zero_at = pieces * cap
    blocks = held * sa
    terms, bufs = (pairs_a, pairs_b), (buf_a, buf_b)

    row = lax.axis_index("row")
    col = lax.axis_index("col")
    layer = lax.axis_index("layer")
    other = 1 - layer
    chips = cols // 2
    sibling = col + 1 - 2 * lax.rem(col, 2)
    twin_id = {"row": row, "col": col, "layer": other}
    sibling_id = {"row": row, "col": sibling, "layer": layer}

    def row_id(at):
        return {"row": at, "col": col, "layer": layer}

    def peer_col(step):
        return lax.rem(col + 2 * step, cols)

    def peer_id(step):
        return {"row": row, "col": peer_col(step), "layer": layer}

    moves = (1, -1)
    reach = [(row + m < rows) if m > 0 else (row + m >= 0) for m in moves]
    aim = [jnp.clip(row + m, 0, rows - 1) for m in moves]

    barrier = pltpu.get_barrier_semaphore()
    greeted = jnp.int32(0)
    for may, at in zip(reach, aim):
        @pl.when(may)
        def _(at=at):
            pl.semaphore_signal(barrier, inc=1, device_id=row_id(at), device_id_type=MESH)

        greeted = greeted + may.astype(jnp.int32)

    for target in (twin_id, sibling_id) + tuple(peer_id(j) for j in range(1, chips)):
        pl.semaphore_signal(barrier, inc=1, device_id=target, device_id_type=MESH)

    own_copies = [
        pltpu.make_async_copy(right_ref, right_in, own_sem.at[0]),
        pltpu.make_async_copy(left_ref, left_in, own_sem.at[1]),
        pltpu.make_async_copy(stacks_ref, lists.at[layer], own_sem.at[2]),
    ]
    for copy in own_copies:
        copy.start()

    def piece(i):
        below, above = row, rows - 1 - row
        near = jnp.minimum(below, above)
        mixed, upward = i <= 2 * near, above > below
        step = jnp.where(mixed, lax.div(i + 1, 2), i - near)
        up = upward ^ (mixed & (lax.rem(i, 2) == 0))
        return jnp.where(up, row + step, row - step)

    def table(t):
        h = jnp.where(t == 0, layer, other)

        def sort_rows(i, carry):
            k = piece(i)
            order_v[t, 0, pl.ds(i, 1), :cap] = lists[h, 2, pl.ds(k, 1)]
            order_v[t, 1, pl.ds(i, 1), :cap] = lists[h, 0, pl.ds(k, 1)] * sb + lists[h, 1, pl.ds(k, 1)]
            return carry

        lax.fori_loop(0, rows, sort_rows, 0)
        out_at = order_v[t, 0, :, :cap]
        place = (lax.broadcasted_iota(jnp.int32, out_at.shape, 0) * cap
                 + lax.broadcasted_iota(jnp.int32, out_at.shape, 1))
        lane = lax.broadcasted_iota(jnp.int32, (1, bs), 1)

        def link(i, carry):
            before, final = carry
            line = order_v[t, 0, pl.ds(i, 1), :cap]
            for q in range(cap):
                mine, spot = line[:, q:q + 1], i * cap + q
                before = jnp.where((out_at == mine) & (place > spot), spot, before)
                final = jnp.where(lane == mine, spot, final)
            return before, final

        before, final = lax.fori_loop(
            0, rows, link,
            (jnp.full(out_at.shape, zero_at, jnp.int32), jnp.full((1, bs), zero_at, jnp.int32)))
        tab_v[t, 0, :, :cap] = order_v[t, 1, :, :cap]
        tab_v[t, 1, :, :cap] = before
        tab_v[t, 2, 0:1] = final
        tab_copy(t).start()

    def tab_copy(t):
        return pltpu.make_async_copy(tab_v.at[t], tab_s.at[t], tab_sem.at[t])

    own_copies[0].wait()
    for b in range(sb):
        turned = right_in[b].T
        low, high = turned[:half], turned[half:]
        keep = jnp.where(layer == 0, low, high)
        give = jnp.where(layer == 0, high, low)
        for n, at in zip(GROUPS, starts):
            slabs[layer, row, sb * at + b * n:sb * at + (b + 1) * n] = keep[at:at + n]
            twin_slab[sb * at + b * n:sb * at + (b + 1) * n] = give[at:at + n]
    own_copies[1].wait()
    for i in range(held):
        for a in range(sa):
            left_all[layer, col * held + i, a] = left_in[i, a].T
    for buf in bufs:
        buf[zero_at] = jnp.zeros_like(buf[zero_at])

    own_copies[2].wait()
    pl.semaphore_wait(barrier, greeted + 1 + chips)

    def remote(src, dst, send, recv, target):
        return pltpu.make_async_remote_copy(
            src_ref=src, dst_ref=dst, send_sem=send, recv_sem=recv,
            device_id=target, device_id_type=MESH)

    def slab(h, k, g):
        return slabs.at[h, k, pl.ds(sb * starts[g], sb * GROUPS[g])]

    def z_copy(way, g, h, k):
        return remote(slab(h, k, g), slab(h, k, g), z_send.at[way, g, h, k], z_recv.at[g, h, k],
                      row_id(aim[way]))

    def sends(way, k):
        return reach[way] & ((k <= row) if moves[way] > 0 else (k >= row))

    def z_forward(g, h, k):
        for way in range(len(moves)):
            @pl.when(sends(way, k))
            def _(way=way):
                z_copy(way, g, h, k).start()

    def z_spread(g, h):
        z_forward(g, h, row)

    def twin_spread(g):
        z_copy(0, g, other, row).wait_recv()
        z_spread(g, other)

    def twin_part(g):
        return remote(twin_slab.at[pl.ds(sb * starts[g], sb * GROUPS[g])], slab(layer, row, g),
                      tw_send.at[g], z_recv.at[g, layer, row], twin_id)

    stack_copy = remote(stacks_ref, lists.at[layer], st_send, st_recv, twin_id)

    def left_slot(h, source, i):
        return left_all.at[h, source * held + i // sa, i % sa]

    def twin_copy(i):
        slot = left_slot(layer, col, i)
        return remote(slot, slot, ly_send.at[i], ly_recv.at[i], twin_id)

    def twin_arrival(i):
        slot = left_slot(other, col, i)
        return remote(slot, slot, ly_send.at[i], ly_recv.at[i], twin_id)

    def left_copy(kind, i, slot):
        source, target = col, sibling_id
        if slot >= chips:
            source = peer_col(cols - slot + chips - 1)
        elif slot:
            target = peer_id(slot)
        at = left_slot(layer if kind == 0 else other, source, i)
        return remote(at, at, lc_send.at[kind, i, slot], lc_recv.at[kind, i, slot], target)

    def left_arrival(kind, i, slot):
        source = sibling
        if slot >= chips:
            source = lax.rem(sibling + 2 * (cols - slot + chips - 1), cols)
        elif slot:
            source = peer_col(cols - slot)
        at = left_slot(layer if kind == 0 else other, source, i)
        return remote(at, at, lc_send.at[kind, i, slot], lc_recv.at[kind, i, slot], sibling_id)

    def relay(kind):
        for i in range(blocks):
            for j in range(1, chips):
                left_arrival(kind, i, j).wait_recv()
                left_copy(kind, i, chips - 1 + j).start()

    z_spread(0, layer)
    stack_copy.start()
    for g in range(FIRST):
        twin_part(g).start()
    for i in range(blocks):
        twin_copy(i).start()
    for i in range(blocks):
        for slot in range(chips - 1, -1, -1):
            left_copy(0, i, slot).start()
    for g in range(1, AHEAD + 1):
        z_spread(g, layer)
    for g in range(FIRST, last + 1):
        twin_part(g).start()

    def pass_on(g, i, twin):
        h = (layer, other)[twin]
        k = piece(i)

        @pl.when((i > 0) & (i < rows))
        def _():
            z_copy(0, g, h, k).wait_recv()
            z_forward(g, h, k)

    def split(value):
        high = value.astype(jnp.bfloat16)
        return high, (value - high.astype(jnp.float32)).astype(jnp.bfloat16)

    def widen(h, k):
        for a in range(sa):
            high, rest = split(left_all[h, k, a])
            wide[h, k, :bs, a * bs:(a + 1) * bs] = high
            wide[h, k, bs:, a * bs:(a + 1) * bs] = rest

    def work(g, i):
        n = GROUPS[g]
        k = piece(i)
        for h, pairs in zip((layer, other), terms):
            if g == 0:
                widen(h, k)
            high, rest = split(slabs[h, k, sb * starts[g]:sb * (starts[g] + n)])
            deep = jnp.concatenate([
                jnp.concatenate([high, high], axis=1), jnp.concatenate([rest, rest], axis=1)], axis=0)
            for a in range(0, sa, 2):
                product = jnp.dot(
                    deep, wide[h, k, :, a * bs:(a + 2) * bs], preferred_element_type=jnp.float32)
                total = product[:sb * n] + product[sb * n:]
                for m in range(2):
                    pairs[(a + m) * sb:(a + m + 1) * sb, :n] = (
                        total[:, m * bs:(m + 1) * bs].reshape(sb, n, bs))

        def chain(q, carry):
            for t, (pairs, buf) in enumerate(zip(terms, bufs)):
                buf[i * cap + q, :n] = pairs[tab_s[t, 0, i, q], :n] + buf[tab_s[t, 1, i, q], :n]
            return carry

        lax.fori_loop(0, cap, chain, 0, unroll=16)

    def summed(o, n):
        return buf_a[tab_s[0, 2, 0, o], :n] + buf_b[tab_s[1, 2, 0, o], :n]

    def exchange(g):
        rng = pl.ds(outs * starts[g], outs * GROUPS[g])
        return remote(theirs.at[rng], mine_out.at[layer, rng], ex_send.at[g], ex_recv.at[g], twin_id)

    def exchanged(g):
        rng = pl.ds(outs * starts[g], outs * GROUPS[g])
        return remote(theirs.at[rng], mine_out.at[other, rng], ex_send.at[g], ex_recv.at[g], twin_id)

    def finish(g):
        n, at = GROUPS[g], outs * starts[g]

        def give(o, carry):
            theirs[pl.ds(pl.multiple_of(at + o * n, 8), n)] = summed(other * outs + o, n)
            return carry

        lax.fori_loop(0, outs, give, 0, unroll=8)
        exchange(g).start()

        def keep(o, carry):
            mine_out[layer, pl.ds(pl.multiple_of(at + o * n, 8), n)] = summed(layer * outs + o, n)
            return carry

        lax.fori_loop(0, outs, keep, 0, unroll=8)

    def run(first, end, passed=None, worked=None):
        later = int(worked is not None and passed != worked)

        def step(i, carry):
            if passed is not None:
                for twin in range(2):
                    pass_on(passed, i + later, twin)
            if worked is not None:
                work(worked, i)
            return carry

        lax.fori_loop(first, end, step, 0)

    def open_group(g):
        z_spread(g, layer)
        twin_spread(g)

    at_end = (row == 0) | (row == rows - 1)
    inside = jnp.logical_not(at_end)
    remote(stacks_ref, lists.at[other], st_send, st_recv, twin_id).wait_recv()

    def tables(t, carry):
        table(t)
        return carry

    lax.fori_loop(0, 2, tables, 0)
    for g in range(EARLY):
        twin_spread(g)

    @pl.when(inside)
    def _():
        run(1, rows // 2 + 1, passed=0)

    relay(0)
    for i in range(blocks):
        twin_arrival(i).wait_recv()
        for slot in range(chips - 1, -1, -1):
            left_copy(1, i, slot).start()
    for g in range(EARLY, AHEAD + 1):
        twin_spread(g)

    @pl.when(inside)
    def _():
        run(rows // 2 + 1, rows, passed=0)

    relay(1)

    @pl.when(inside)
    def _():
        for g in range(1, LEAD):
            run(1, rows, passed=g)

    for kind in range(2):
        for i in range(blocks):
            for slot in (0,) + tuple(range(chips, cols - 1)):
                left_arrival(kind, i, slot).wait_recv()
    for t in range(2):
        tab_copy(t).wait()

    @pl.when(at_end)
    def _():
        for g in range(last + 1):
            if g and g + AHEAD <= last:
                open_group(g + AHEAD)
            run(0, rows, passed=g, worked=g)
            finish(g)

    @pl.when(inside)
    def _():
        for g in range(last + 1):
            ahead = g + LEAD
            if ahead + AHEAD <= last:
                open_group(ahead + AHEAD)
            run(0, rows, passed=ahead if ahead <= last else None, worked=g)
            finish(g)

    def drain(s, carry):
        h, k = lax.rem(s, 2), lax.div(s, 2)

        for way in range(len(moves)):
            @pl.when(sends(way, k))
            def _(way=way):
                for g in range(last + 1):
                    z_copy(way, g, h, k).wait_send()

        return carry

    lax.fori_loop(0, 2 * rows, drain, 0)
    stack_copy.wait_send()
    for i in range(blocks):
        twin_copy(i).wait_send()
        for kind in range(2):
            for slot in range(cols - 1):
                left_copy(kind, i, slot).wait_send()
    for g in range(last + 1):
        twin_part(g).wait_send()
        exchange(g).wait_send()
    for g in range(last + 1):
        exchanged(g).wait_recv()


def turn(parts_ref, out_ref, held, sems):
    outs = out_ref.shape[0]
    starts = tuple(sum(GROUPS[:g]) for g in range(len(GROUPS)))
    copies = []
    for o in range(outs):
        held[o] = jnp.concatenate([
            parts_ref[side, outs * at + o * n:outs * at + (o + 1) * n]
            for side in range(2) for n, at in zip(GROUPS, starts)], axis=0).T
        copies.append(pltpu.make_async_copy(held.at[o], out_ref.at[o], sems.at[o]))
        copies[-1].start()
    for copy in copies:
        copy.wait()


def body(rows, cols, left_blocks, right_blocks, pair_stacks):
    left_local = left_blocks[0, 0]
    right_local = right_blocks[0, 0, 0]
    stacks = jnp.swapaxes(pair_stacks[0, 0, 0], 0, 1)
    held, sa, bs, _ = left_local.shape
    sb = right_local.shape[0]
    _, pieces, cap = stacks.shape
    outs = OUT_TILE // 2
    parts = len(GROUPS)
    tall = max(GROUPS)
    half = bs // 2
    f32 = jnp.float32
    dma = pltpu.SemaphoreType.DMA
    vmem = pl.BlockSpec(memory_space=pltpu.VMEM)
    places = pieces * cap + 1
    scratch = [
        ((held, sa, bs, bs), f32),
        ((sb, bs, bs), f32),
        ((2, pieces, sa, bs, bs), f32),
        ((2, pieces, sb * half, bs), f32),
        ((sb * half, bs), f32),
        ((2, 3, pieces, cap), jnp.int32),
        ((2, 2, pieces, bs), jnp.int32),
        ((2, 3, pieces, bs), jnp.int32),
        ((2, pieces, 2 * bs, sa * bs), jnp.bfloat16),
        ((sa * sb, tall, bs), f32),
        ((sa * sb, tall, bs), f32),
        ((places, tall, bs), f32),
        ((places, tall, bs), f32),
        ((outs * half, bs), f32),
    ]
    size = outs * bs * bs * 4
    for shape, kind in scratch:
        count = 1
        for d in shape:
            count *= d
        size += count * jnp.dtype(kind).itemsize
    refs = [pltpu.VMEM(shape, kind) for shape, kind in scratch]
    refs.insert(8, pltpu.SMEM((2, 3, pieces, bs), jnp.int32))
    result = pl.pallas_call(
        functools.partial(kernel, rows, cols),
        out_shape=jax.ShapeDtypeStruct((2, outs * half, bs), f32),
        in_specs=[pl.BlockSpec(memory_space=pltpu.HBM)] * 3,
        out_specs=vmem,
        scratch_shapes=refs + [
            dma((2, parts, 2, pieces)),
            dma((parts, 2, pieces)),
            dma((parts,)),
            dma((parts,)),
            dma((parts,)),
            dma((held * sa,)),
            dma((held * sa,)),
            dma((2, held * sa, cols - 1)),
            dma((2, held * sa, cols - 1)),
            dma, dma,
            dma((2,)),
            dma((3,)),
        ],
        compiler_params=pltpu.CompilerParams(
            collective_id=0, has_side_effects=True, vmem_limit_bytes=size + (6 << 20)),
        name="column_window",
    )(*(pltpu.with_memory_space_constraint(v, pltpu.HBM) for v in (left_local, right_local, stacks)))
    turned = pl.pallas_call(
        turn,
        out_shape=jax.ShapeDtypeStruct((outs, bs, bs), f32),
        in_specs=[vmem],
        out_specs=pl.BlockSpec(memory_space=pltpu.HBM),
        scratch_shapes=[pltpu.VMEM((outs, bs, bs), f32), dma((outs,))],
        compiler_params=pltpu.CompilerParams(vmem_limit_bytes=8 << 20),
        name="turn",
    )(result)
    return turned[None, None]


def solution(mesh):
    placed = (
        P("row", "layer", "col", None, None, None),
        P("layer", "row", "col", None, None, None),
        P("row", "col", "layer", None, None, None),
    )
    return jax.shard_map(
        functools.partial(body, mesh.shape["row"], mesh.shape["col"]),
        mesh=mesh,
        in_specs=placed,
        out_specs=P("row", "col", "layer", None, None),
        check_vma=False,
    )
```

```python
import functools

import jax
import jax.numpy as jnp
from jax import lax
from jax.experimental import pallas as pl
from jax.experimental.pallas import tpu as pltpu
from jax.sharding import PartitionSpec as P

OUT_TILE = 32
GROUPS = (32, 16, 8, 8)
AHEAD = 3
FIRST = 2
EARLY = 2
LEAD = 2
MESH = pl.DeviceIdType.MESH


def kernel(
    rows, cols, left_ref, right_ref, stacks_ref, out_ref,
    left_in, right_in, left_all, slabs, twin_slab, lists, order_v, tab_v, tab_s,
    wide, pairs_a, pairs_b, buf_a, buf_b, theirs,
    z_send, z_recv, tw_send, ex_send, ex_recv, ly_send, ly_recv, lc_send, lc_recv,
    st_send, st_recv, tab_sem, own_sem,
):
    held, sa, bs, _ = left_ref.shape
    sb = right_ref.shape[0]
    _, pieces, cap = stacks_ref.shape
    outs = OUT_TILE // 2
    mine_out = out_ref
    half = bs // 2
    starts = tuple(sum(GROUPS[:g]) for g in range(len(GROUPS)))
    last = len(GROUPS) - 1
    zero_at = pieces * cap
    blocks = held * sa
    terms, bufs = (pairs_a, pairs_b), (buf_a, buf_b)

    row = lax.axis_index("row")
    col = lax.axis_index("col")
    layer = lax.axis_index("layer")
    other = 1 - layer
    chips = cols // 2
    sibling = col + 1 - 2 * lax.rem(col, 2)
    twin_id = {"row": row, "col": col, "layer": other}
    sibling_id = {"row": row, "col": sibling, "layer": layer}

    def row_id(at):
        return {"row": at, "col": col, "layer": layer}

    def peer_col(step):
        return lax.rem(col + 2 * step, cols)

    def peer_id(step):
        return {"row": row, "col": peer_col(step), "layer": layer}

    moves = (1, -1)
    reach = [(row + m < rows) if m > 0 else (row + m >= 0) for m in moves]
    aim = [jnp.clip(row + m, 0, rows - 1) for m in moves]

    barrier = pltpu.get_barrier_semaphore()
    greeted = jnp.int32(0)
    for may, at in zip(reach, aim):
        @pl.when(may)
        def _(at=at):
            pl.semaphore_signal(barrier, inc=1, device_id=row_id(at), device_id_type=MESH)

        greeted = greeted + may.astype(jnp.int32)

    for target in (twin_id, sibling_id) + tuple(peer_id(j) for j in range(1, chips)):
        pl.semaphore_signal(barrier, inc=1, device_id=target, device_id_type=MESH)

    own_copies = [
        pltpu.make_async_copy(right_ref, right_in, own_sem.at[0]),
        pltpu.make_async_copy(left_ref, left_in, own_sem.at[1]),
        pltpu.make_async_copy(stacks_ref, lists.at[layer], own_sem.at[2]),
    ]
    for copy in own_copies:
        copy.start()

    def piece(i):
        below, above = row, rows - 1 - row
        near = jnp.minimum(below, above)
        mixed, upward = i <= 2 * near, above > below
        step = jnp.where(mixed, lax.div(i + 1, 2), i - near)
        up = upward ^ (mixed & (lax.rem(i, 2) == 0))
        return jnp.where(up, row + step, row - step)

    def table(t):
        h = jnp.where(t == 0, layer, other)

        def sort_rows(i, carry):
            k = piece(i)
            order_v[t, 0, pl.ds(i, 1), :cap] = lists[h, 2, pl.ds(k, 1)]
            order_v[t, 1, pl.ds(i, 1), :cap] = lists[h, 0, pl.ds(k, 1)] * sb + lists[h, 1, pl.ds(k, 1)]
            return carry

        lax.fori_loop(0, rows, sort_rows, 0)
        out_at = order_v[t, 0, :, :cap]
        place = (lax.broadcasted_iota(jnp.int32, out_at.shape, 0) * cap
                 + lax.broadcasted_iota(jnp.int32, out_at.shape, 1))
        lane = lax.broadcasted_iota(jnp.int32, (1, bs), 1)

        def link(i, carry):
            before, final = carry
            line = order_v[t, 0, pl.ds(i, 1), :cap]
            for q in range(cap):
                mine, spot = line[:, q:q + 1], i * cap + q
                before = jnp.where((out_at == mine) & (place > spot), spot, before)
                final = jnp.where(lane == mine, spot, final)
            return before, final

        before, final = lax.fori_loop(
            0, rows, link,
            (jnp.full(out_at.shape, zero_at, jnp.int32), jnp.full((1, bs), zero_at, jnp.int32)))
        tab_v[t, 0, :, :cap] = order_v[t, 1, :, :cap]
        tab_v[t, 1, :, :cap] = before
        tab_v[t, 2, 0:1] = final
        tab_copy(t).start()

    def tab_copy(t):
        return pltpu.make_async_copy(tab_v.at[t], tab_s.at[t], tab_sem.at[t])

    own_copies[0].wait()
    for b in range(sb):
        turned = right_in[b].T
        low, high = turned[:half], turned[half:]
        keep = jnp.where(layer == 0, low, high)
        give = jnp.where(layer == 0, high, low)
        for n, at in zip(GROUPS, starts):
            slabs[layer, row, sb * at + b * n:sb * at + (b + 1) * n] = keep[at:at + n]
            twin_slab[sb * at + b * n:sb * at + (b + 1) * n] = give[at:at + n]
    own_copies[1].wait()
    for i in range(held):
        for a in range(sa):
            left_all[layer, col * held + i, a] = left_in[i, a].T
    for buf in bufs:
        buf[zero_at] = jnp.zeros_like(buf[zero_at])

    own_copies[2].wait()
    pl.semaphore_wait(barrier, greeted + 1 + chips)

    def remote(src, dst, send, recv, target):
        return pltpu.make_async_remote_copy(
            src_ref=src, dst_ref=dst, send_sem=send, recv_sem=recv,
            device_id=target, device_id_type=MESH)

    def slab(h, k, g):
        return slabs.at[h, k, pl.ds(sb * starts[g], sb * GROUPS[g])]

    def z_copy(way, g, h, k):
        return remote(slab(h, k, g), slab(h, k, g), z_send.at[way, g, h, k], z_recv.at[g, h, k],
                      row_id(aim[way]))

    def sends(way, k):
        return reach[way] & ((k <= row) if moves[way] > 0 else (k >= row))

    def z_forward(g, h, k):
        for way in range(len(moves)):
            @pl.when(sends(way, k))
            def _(way=way):
                z_copy(way, g, h, k).start()

    def z_spread(g, h):
        z_forward(g, h, row)

    def twin_spread(g):
        z_copy(0, g, other, row).wait_recv()
        z_spread(g, other)

    def twin_part(g):
        return remote(twin_slab.at[pl.ds(sb * starts[g], sb * GROUPS[g])], slab(layer, row, g),
                      tw_send.at[g], z_recv.at[g, layer, row], twin_id)

    stack_copy = remote(stacks_ref, lists.at[layer], st_send, st_recv, twin_id)

    def left_slot(h, source, i):
        return left_all.at[h, source * held + i // sa, i % sa]

    def twin_copy(i):
        slot = left_slot(layer, col, i)
        return remote(slot, slot, ly_send.at[i], ly_recv.at[i], twin_id)

    def twin_arrival(i):
        slot = left_slot(other, col, i)
        return remote(slot, slot, ly_send.at[i], ly_recv.at[i], twin_id)

    def left_copy(kind, i, slot):
        source, target = col, sibling_id
        if slot >= chips:
            source = peer_col(cols - slot + chips - 1)
        elif slot:
            target = peer_id(slot)
        at = left_slot(layer if kind == 0 else other, source, i)
        return remote(at, at, lc_send.at[kind, i, slot], lc_recv.at[kind, i, slot], target)

    def left_arrival(kind, i, slot):
        source = sibling
        if slot >= chips:
            source = lax.rem(sibling + 2 * (cols - slot + chips - 1), cols)
        elif slot:
            source = peer_col(cols - slot)
        at = left_slot(layer if kind == 0 else other, source, i)
        return remote(at, at, lc_send.at[kind, i, slot], lc_recv.at[kind, i, slot], sibling_id)

    def relay(kind):
        for i in range(blocks):
            for j in range(1, chips):
                left_arrival(kind, i, j).wait_recv()
                left_copy(kind, i, chips - 1 + j).start()

    z_spread(0, layer)
    stack_copy.start()
    for g in range(FIRST):
        twin_part(g).start()
    for i in range(blocks):
        twin_copy(i).start()
    for i in range(blocks):
        for slot in range(chips - 1, -1, -1):
            left_copy(0, i, slot).start()
    for g in range(1, AHEAD + 1):
        z_spread(g, layer)
    for g in range(FIRST, last + 1):
        twin_part(g).start()

    def pass_on(g, i, twin):
        h = (layer, other)[twin]
        k = piece(i)

        @pl.when((i > 0) & (i < rows))
        def _():
            z_copy(0, g, h, k).wait_recv()
            z_forward(g, h, k)

    def split(value):
        high = value.astype(jnp.bfloat16)
        return high, (value - high.astype(jnp.float32)).astype(jnp.bfloat16)

    def widen(h, k):
        for a in range(sa):
            high, rest = split(left_all[h, k, a])
            wide[h, k, :bs, a * bs:(a + 1) * bs] = high
            wide[h, k, bs:, a * bs:(a + 1) * bs] = rest

    def work(g, i):
        n = GROUPS[g]
        k = piece(i)
        for h, pairs in zip((layer, other), terms):
            if g == 0:
                widen(h, k)
            high, rest = split(slabs[h, k, sb * starts[g]:sb * (starts[g] + n)])
            deep = jnp.concatenate([
                jnp.concatenate([high, high], axis=1), jnp.concatenate([rest, rest], axis=1)], axis=0)
            for a in range(0, sa, 2):
                product = jnp.dot(
                    deep, wide[h, k, :, a * bs:(a + 2) * bs], preferred_element_type=jnp.float32)
                total = product[:sb * n] + product[sb * n:]
                for m in range(2):
                    pairs[(a + m) * sb:(a + m + 1) * sb, :n] = (
                        total[:, m * bs:(m + 1) * bs].reshape(sb, n, bs))

        def chain(q, carry):
            for t, (pairs, buf) in enumerate(zip(terms, bufs)):
                buf[i * cap + q, :n] = pairs[tab_s[t, 0, i, q], :n] + buf[tab_s[t, 1, i, q], :n]
            return carry

        lax.fori_loop(0, cap, chain, 0, unroll=32)

    def summed(o, n):
        return buf_a[tab_s[0, 2, 0, o], :n] + buf_b[tab_s[1, 2, 0, o], :n]

    def exchange(g):
        rng = pl.ds(outs * starts[g], outs * GROUPS[g])
        return remote(theirs.at[rng], mine_out.at[layer, rng], ex_send.at[g], ex_recv.at[g], twin_id)

    def exchanged(g):
        rng = pl.ds(outs * starts[g], outs * GROUPS[g])
        return remote(theirs.at[rng], mine_out.at[other, rng], ex_send.at[g], ex_recv.at[g], twin_id)

    def finish(g):
        n, at = GROUPS[g], outs * starts[g]

        def give(o, carry):
            theirs[pl.ds(pl.multiple_of(at + o * n, 8), n)] = summed(other * outs + o, n)
            return carry

        lax.fori_loop(0, outs, give, 0, unroll=8)
        exchange(g).start()

        def keep(o, carry):
            mine_out[layer, pl.ds(pl.multiple_of(at + o * n, 8), n)] = summed(layer * outs + o, n)
            return carry

        lax.fori_loop(0, outs, keep, 0, unroll=8)

    def run(first, end, passed=None, worked=None):
        later = int(worked is not None and passed != worked)

        def step(i, carry):
            if passed is not None:
                for twin in range(2):
                    pass_on(passed, i + later, twin)
            if worked is not None:
                work(worked, i)
            return carry

        lax.fori_loop(first, end, step, 0)

    def open_group(g):
        z_spread(g, layer)
        twin_spread(g)

    at_end = (row == 0) | (row == rows - 1)
    inside = jnp.logical_not(at_end)
    remote(stacks_ref, lists.at[other], st_send, st_recv, twin_id).wait_recv()

    def tables(t, carry):
        table(t)
        return carry

    lax.fori_loop(0, 2, tables, 0)
    for g in range(EARLY):
        twin_spread(g)

    @pl.when(inside)
    def _():
        run(1, rows // 2 + 1, passed=0)

    relay(0)
    for i in range(blocks):
        twin_arrival(i).wait_recv()
        for slot in range(chips - 1, -1, -1):
            left_copy(1, i, slot).start()
    for g in range(EARLY, AHEAD + 1):
        twin_spread(g)

    @pl.when(inside)
    def _():
        run(rows // 2 + 1, rows, passed=0)

    relay(1)

    @pl.when(inside)
    def _():
        for g in range(1, LEAD):
            run(1, rows, passed=g)

    for kind in range(2):
        for i in range(blocks):
            for slot in (0,) + tuple(range(chips, cols - 1)):
                left_arrival(kind, i, slot).wait_recv()
    for t in range(2):
        tab_copy(t).wait()

    @pl.when(at_end)
    def _():
        for g in range(last + 1):
            if g and g + AHEAD <= last:
                open_group(g + AHEAD)
            run(0, rows, passed=g, worked=g)
            finish(g)

    @pl.when(inside)
    def _():
        for g in range(last + 1):
            ahead = g + LEAD
            if ahead + AHEAD <= last:
                open_group(ahead + AHEAD)
            run(0, rows, passed=ahead if ahead <= last else None, worked=g)
            finish(g)

    def drain(s, carry):
        h, k = lax.rem(s, 2), lax.div(s, 2)

        for way in range(len(moves)):
            @pl.when(sends(way, k))
            def _(way=way):
                for g in range(last + 1):
                    z_copy(way, g, h, k).wait_send()

        return carry

    lax.fori_loop(0, 2 * rows, drain, 0)
    stack_copy.wait_send()
    for i in range(blocks):
        twin_copy(i).wait_send()
        for kind in range(2):
            for slot in range(cols - 1):
                left_copy(kind, i, slot).wait_send()
    for g in range(last + 1):
        twin_part(g).wait_send()
        exchange(g).wait_send()
    for g in range(last + 1):
        exchanged(g).wait_recv()


def turn(parts_ref, out_ref, held, sems):
    outs = out_ref.shape[0]
    starts = tuple(sum(GROUPS[:g]) for g in range(len(GROUPS)))
    copies = []
    for o in range(outs):
        held[o] = jnp.concatenate([
            parts_ref[side, outs * at + o * n:outs * at + (o + 1) * n]
            for side in range(2) for n, at in zip(GROUPS, starts)], axis=0).T
        copies.append(pltpu.make_async_copy(held.at[o], out_ref.at[o], sems.at[o]))
        copies[-1].start()
    for copy in copies:
        copy.wait()


def body(rows, cols, left_blocks, right_blocks, pair_stacks):
    left_local = left_blocks[0, 0]
    right_local = right_blocks[0, 0, 0]
    stacks = jnp.swapaxes(pair_stacks[0, 0, 0], 0, 1)
    held, sa, bs, _ = left_local.shape
    sb = right_local.shape[0]
    _, pieces, cap = stacks.shape
    outs = OUT_TILE // 2
    parts = len(GROUPS)
    tall = max(GROUPS)
    half = bs // 2
    f32 = jnp.float32
    dma = pltpu.SemaphoreType.DMA
    vmem = pl.BlockSpec(memory_space=pltpu.VMEM)
    places = pieces * cap + 1
    scratch = [
        ((held, sa, bs, bs), f32),
        ((sb, bs, bs), f32),
        ((2, pieces, sa, bs, bs), f32),
        ((2, pieces, sb * half, bs), f32),
        ((sb * half, bs), f32),
        ((2, 3, pieces, cap), jnp.int32),
        ((2, 2, pieces, bs), jnp.int32),
        ((2, 3, pieces, bs), jnp.int32),
        ((2, pieces, 2 * bs, sa * bs), jnp.bfloat16),
        ((sa * sb, tall, bs), f32),
        ((sa * sb, tall, bs), f32),
        ((places, tall, bs), f32),
        ((places, tall, bs), f32),
        ((outs * half, bs), f32),
    ]
    size = outs * bs * bs * 4
    for shape, kind in scratch:
        count = 1
        for d in shape:
            count *= d
        size += count * jnp.dtype(kind).itemsize
    refs = [pltpu.VMEM(shape, kind) for shape, kind in scratch]
    refs.insert(8, pltpu.SMEM((2, 3, pieces, bs), jnp.int32))
    result = pl.pallas_call(
        functools.partial(kernel, rows, cols),
        out_shape=jax.ShapeDtypeStruct((2, outs * half, bs), f32),
        in_specs=[pl.BlockSpec(memory_space=pltpu.HBM)] * 3,
        out_specs=vmem,
        scratch_shapes=refs + [
            dma((2, parts, 2, pieces)),
            dma((parts, 2, pieces)),
            dma((parts,)),
            dma((parts,)),
            dma((parts,)),
            dma((held * sa,)),
            dma((held * sa,)),
            dma((2, held * sa, cols - 1)),
            dma((2, held * sa, cols - 1)),
            dma, dma,
            dma((2,)),
            dma((3,)),
        ],
        compiler_params=pltpu.CompilerParams(
            collective_id=0, has_side_effects=True, vmem_limit_bytes=size + (6 << 20)),
        name="column_window",
    )(*(pltpu.with_memory_space_constraint(v, pltpu.HBM) for v in (left_local, right_local, stacks)))
    turned = pl.pallas_call(
        turn,
        out_shape=jax.ShapeDtypeStruct((outs, bs, bs), f32),
        in_specs=[vmem],
        out_specs=pl.BlockSpec(memory_space=pltpu.HBM),
        scratch_shapes=[pltpu.VMEM((outs, bs, bs), f32), dma((outs,))],
        compiler_params=pltpu.CompilerParams(vmem_limit_bytes=8 << 20),
        name="turn",
    )(result)
    return turned[None, None]


def solution(mesh):
    placed = (
        P("row", "layer", "col", None, None, None),
        P("layer", "row", "col", None, None, None),
        P("row", "col", "layer", None, None, None),
    )
    return jax.shard_map(
        functools.partial(body, mesh.shape["row"], mesh.shape["col"]),
        mesh=mesh,
        in_specs=placed,
        out_specs=P("row", "col", "layer", None, None),
        check_vma=False,
    )
```

```python
import functools

import jax
import jax.numpy as jnp
from jax import lax
from jax.experimental import pallas as pl
from jax.experimental.pallas import tpu as pltpu
from jax.sharding import PartitionSpec as P

OUT_TILE = 32
GROUPS = (32, 16, 8, 8)
AHEAD = 3
FIRST = 2
EARLY = 2
LEAD = 2
MESH = pl.DeviceIdType.MESH


def kernel(
    rows, cols, left_ref, right_ref, stacks_ref, out_ref,
    left_in, right_in, left_all, slabs, twin_slab, lists, order_v, tab_v, tab_s,
    wide, pairs_a, pairs_b, buf_a, buf_b, theirs,
    z_send, z_recv, tw_send, ex_send, ex_recv, ly_send, ly_recv, lc_send, lc_recv,
    st_send, st_recv, tab_sem, own_sem,
):
    held, sa, bs, _ = left_ref.shape
    sb = right_ref.shape[0]
    _, pieces, cap = stacks_ref.shape
    outs = OUT_TILE // 2
    mine_out = out_ref
    half = bs // 2
    starts = tuple(sum(GROUPS[:g]) for g in range(len(GROUPS)))
    last = len(GROUPS) - 1
    zero_at = pieces * cap
    blocks = held * sa
    terms, bufs = (pairs_a, pairs_b), (buf_a, buf_b)

    row = lax.axis_index("row")
    col = lax.axis_index("col")
    layer = lax.axis_index("layer")
    other = 1 - layer
    chips = cols // 2
    sibling = col + 1 - 2 * lax.rem(col, 2)
    twin_id = {"row": row, "col": col, "layer": other}
    sibling_id = {"row": row, "col": sibling, "layer": layer}

    def row_id(at):
        return {"row": at, "col": col, "layer": layer}

    def peer_col(step):
        return lax.rem(col + 2 * step, cols)

    def peer_id(step):
        return {"row": row, "col": peer_col(step), "layer": layer}

    moves = (1, -1)
    reach = [(row + m < rows) if m > 0 else (row + m >= 0) for m in moves]
    aim = [jnp.clip(row + m, 0, rows - 1) for m in moves]

    barrier = pltpu.get_barrier_semaphore()
    greeted = jnp.int32(0)
    for may, at in zip(reach, aim):
        @pl.when(may)
        def _(at=at):
            pl.semaphore_signal(barrier, inc=1, device_id=row_id(at), device_id_type=MESH)

        greeted = greeted + may.astype(jnp.int32)

    for target in (twin_id, sibling_id) + tuple(peer_id(j) for j in range(1, chips)):
        pl.semaphore_signal(barrier, inc=1, device_id=target, device_id_type=MESH)

    own_copies = [
        pltpu.make_async_copy(right_ref, right_in, own_sem.at[0]),
        pltpu.make_async_copy(left_ref, left_in, own_sem.at[1]),
        pltpu.make_async_copy(stacks_ref, lists.at[layer], own_sem.at[2]),
    ]
    for copy in own_copies:
        copy.start()

    def piece(i):
        below, above = row, rows - 1 - row
        near = jnp.minimum(below, above)
        mixed, upward = i <= 2 * near, above > below
        step = jnp.where(mixed, lax.div(i + 1, 2), i - near)
        up = upward ^ (mixed & (lax.rem(i, 2) == 0))
        return jnp.where(up, row + step, row - step)

    def table(t):
        h = jnp.where(t == 0, layer, other)

        def sort_rows(i, carry):
            k = piece(i)
            order_v[t, 0, pl.ds(i, 1), :cap] = lists[h, 2, pl.ds(k, 1)]
            order_v[t, 1, pl.ds(i, 1), :cap] = lists[h, 0, pl.ds(k, 1)] * sb + lists[h, 1, pl.ds(k, 1)]
            return carry

        lax.fori_loop(0, rows, sort_rows, 0)
        out_at = order_v[t, 0, :, :cap]
        place = (lax.broadcasted_iota(jnp.int32, out_at.shape, 0) * cap
                 + lax.broadcasted_iota(jnp.int32, out_at.shape, 1))
        lane = lax.broadcasted_iota(jnp.int32, (1, bs), 1)

        def link(i, carry):
            before, final = carry
            line = order_v[t, 0, pl.ds(i, 1), :cap]
            for q in range(cap):
                mine, spot = line[:, q:q + 1], i * cap + q
                before = jnp.where((out_at == mine) & (place > spot), spot, before)
                final = jnp.where(lane == mine, spot, final)
            return before, final

        before, final = lax.fori_loop(
            0, rows, link,
            (jnp.full(out_at.shape, zero_at, jnp.int32), jnp.full((1, bs), zero_at, jnp.int32)))
        tab_v[t, 0, :, :cap] = order_v[t, 1, :, :cap]
        tab_v[t, 1, :, :cap] = before
        tab_v[t, 2, 0:1] = final
        tab_copy(t).start()

    def tab_copy(t):
        return pltpu.make_async_copy(tab_v.at[t], tab_s.at[t], tab_sem.at[t])

    own_copies[0].wait()
    for b in range(sb):
        turned = right_in[b].T
        low, high = turned[:half], turned[half:]
        keep = jnp.where(layer == 0, low, high)
        give = jnp.where(layer == 0, high, low)
        for n, at in zip(GROUPS, starts):
            slabs[layer, row, sb * at + b * n:sb * at + (b + 1) * n] = keep[at:at + n]
            twin_slab[sb * at + b * n:sb * at + (b + 1) * n] = give[at:at + n]
    own_copies[1].wait()
    for i in range(held):
        for a in range(sa):
            left_all[layer, col * held + i, a] = left_in[i, a].T
    for buf in bufs:
        buf[zero_at] = jnp.zeros_like(buf[zero_at])

    own_copies[2].wait()
    pl.semaphore_wait(barrier, greeted + 1 + chips)

    def remote(src, dst, send, recv, target):
        return pltpu.make_async_remote_copy(
            src_ref=src, dst_ref=dst, send_sem=send, recv_sem=recv,
            device_id=target, device_id_type=MESH)

    def slab(h, k, g):
        return slabs.at[h, k, pl.ds(sb * starts[g], sb * GROUPS[g])]

    def z_copy(way, g, h, k):
        return remote(slab(h, k, g), slab(h, k, g), z_send.at[way, g, h, k], z_recv.at[g, h, k],
                      row_id(aim[way]))

    def sends(way, k):
        return reach[way] & ((k <= row) if moves[way] > 0 else (k >= row))

    def z_forward(g, h, k):
        for way in range(len(moves)):
            @pl.when(sends(way, k))
            def _(way=way):
                z_copy(way, g, h, k).start()

    def z_spread(g, h):
        z_forward(g, h, row)

    def twin_spread(g):
        z_copy(0, g, other, row).wait_recv()
        z_spread(g, other)

    def twin_part(g):
        return remote(twin_slab.at[pl.ds(sb * starts[g], sb * GROUPS[g])], slab(layer, row, g),
                      tw_send.at[g], z_recv.at[g, layer, row], twin_id)

    stack_copy = remote(stacks_ref, lists.at[layer], st_send, st_recv, twin_id)

    def left_slot(h, source, i):
        return left_all.at[h, source * held + i // sa, i % sa]

    def twin_copy(i):
        slot = left_slot(layer, col, i)
        return remote(slot, slot, ly_send.at[i], ly_recv.at[i], twin_id)

    def twin_arrival(i):
        slot = left_slot(other, col, i)
        return remote(slot, slot, ly_send.at[i], ly_recv.at[i], twin_id)

    def left_copy(kind, i, slot):
        source, target = col, sibling_id
        if slot >= chips:
            source = peer_col(cols - slot + chips - 1)
        elif slot:
            target = peer_id(slot)
        at = left_slot(layer if kind == 0 else other, source, i)
        return remote(at, at, lc_send.at[kind, i, slot], lc_recv.at[kind, i, slot], target)

    def left_arrival(kind, i, slot):
        source = sibling
        if slot >= chips:
            source = lax.rem(sibling + 2 * (cols - slot + chips - 1), cols)
        elif slot:
            source = peer_col(cols - slot)
        at = left_slot(layer if kind == 0 else other, source, i)
        return remote(at, at, lc_send.at[kind, i, slot], lc_recv.at[kind, i, slot], sibling_id)

    def relay(kind):
        for i in range(blocks):
            for j in range(1, chips):
                left_arrival(kind, i, j).wait_recv()
                left_copy(kind, i, chips - 1 + j).start()

    z_spread(0, layer)
    stack_copy.start()
    for g in range(FIRST):
        twin_part(g).start()
    for i in range(blocks):
        twin_copy(i).start()
    for i in range(blocks):
        for slot in range(chips - 1, -1, -1):
            left_copy(0, i, slot).start()
    for g in range(1, AHEAD + 1):
        z_spread(g, layer)
    for g in range(FIRST, last + 1):
        twin_part(g).start()

    def pass_on(g, i, twin):
        h = (layer, other)[twin]
        k = piece(i)

        @pl.when((i > 0) & (i < rows))
        def _():
            z_copy(0, g, h, k).wait_recv()
            z_forward(g, h, k)

    def split(value):
        high = value.astype(jnp.bfloat16)
        return high, (value - high.astype(jnp.float32)).astype(jnp.bfloat16)

    def widen(h, k):
        for a in range(sa):
            high, rest = split(left_all[h, k, a])
            wide[h, k, :bs, a * bs:(a + 1) * bs] = high
            wide[h, k, bs:, a * bs:(a + 1) * bs] = rest

    def work(g, i):
        n = GROUPS[g]
        k = piece(i)
        for h, pairs in zip((layer, other), terms):
            if g == 0:
                widen(h, k)
            high, rest = split(slabs[h, k, sb * starts[g]:sb * (starts[g] + n)])
            deep = jnp.concatenate([
                jnp.concatenate([high, high], axis=1), jnp.concatenate([rest, rest], axis=1)], axis=0)
            for a in range(0, sa, 2):
                product = jnp.dot(
                    deep, wide[h, k, :, a * bs:(a + 2) * bs], preferred_element_type=jnp.float32)
                total = product[:sb * n] + product[sb * n:]
                for m in range(2):
                    pairs[(a + m) * sb:(a + m + 1) * sb, :n] = (
                        total[:, m * bs:(m + 1) * bs].reshape(sb, n, bs))

        def chain(q, carry):
            for t, (pairs, buf) in enumerate(zip(terms, bufs)):
                buf[i * cap + q, :n] = pairs[tab_s[t, 0, i, q], :n] + buf[tab_s[t, 1, i, q], :n]
            return carry

        lax.fori_loop(0, cap, chain, 0, unroll=32)

    def summed(o, n):
        return buf_a[tab_s[0, 2, 0, o], :n] + buf_b[tab_s[1, 2, 0, o], :n]

    def exchange(g):
        rng = pl.ds(outs * starts[g], outs * GROUPS[g])
        return remote(theirs.at[rng], mine_out.at[layer, rng], ex_send.at[g], ex_recv.at[g], twin_id)

    def exchanged(g):
        rng = pl.ds(outs * starts[g], outs * GROUPS[g])
        return remote(theirs.at[rng], mine_out.at[other, rng], ex_send.at[g], ex_recv.at[g], twin_id)

    def finish(g):
        n, at = GROUPS[g], outs * starts[g]

        def give(o, carry):
            theirs[pl.ds(pl.multiple_of(at + o * n, 8), n)] = summed(other * outs + o, n)
            return carry

        lax.fori_loop(0, outs, give, 0, unroll=8)
        exchange(g).start()

        def keep(o, carry):
            mine_out[layer, pl.ds(pl.multiple_of(at + o * n, 8), n)] = summed(layer * outs + o, n)
            return carry

        lax.fori_loop(0, outs, keep, 0, unroll=8)

    def run(first, end, passed=None, worked=None):
        later = int(worked is not None and passed != worked)

        def step(i, carry):
            if passed is not None:
                for twin in range(2):
                    pass_on(passed, i + later, twin)
            if worked is not None:
                work(worked, i)
            return carry

        lax.fori_loop(first, end, step, 0)

    def open_group(g):
        z_spread(g, layer)
        twin_spread(g)

    at_end = (row == 0) | (row == rows - 1)
    inside = jnp.logical_not(at_end)
    remote(stacks_ref, lists.at[other], st_send, st_recv, twin_id).wait_recv()

    def tables(t, carry):
        table(t)
        return carry

    lax.fori_loop(0, 2, tables, 0)
    for g in range(EARLY):
        twin_spread(g)

    @pl.when(inside)
    def _():
        run(1, rows // 2 + 1, passed=0)

    relay(0)
    for i in range(blocks):
        twin_arrival(i).wait_recv()
        for slot in range(chips - 1, -1, -1):
            left_copy(1, i, slot).start()
    for g in range(EARLY, AHEAD + 1):
        twin_spread(g)

    @pl.when(inside)
    def _():
        run(rows // 2 + 1, rows, passed=0)

    relay(1)

    @pl.when(inside)
    def _():
        for g in range(1, LEAD):
            run(1, rows, passed=g)

    for kind in range(2):
        for i in range(blocks):
            for slot in (0,) + tuple(range(chips, cols - 1)):
                left_arrival(kind, i, slot).wait_recv()
    for t in range(2):
        tab_copy(t).wait()

    @pl.when(at_end)
    def _():
        for g in range(last + 1):
            if g and g + AHEAD <= last:
                open_group(g + AHEAD)
            run(0, rows, passed=g, worked=g)
            finish(g)

    @pl.when(inside)
    def _():
        for g in range(last + 1):
            ahead = g + LEAD
            if ahead + AHEAD <= last:
                open_group(ahead + AHEAD)
            run(0, rows, passed=ahead if ahead <= last else None, worked=g)
            finish(g)

    def drain(s, carry):
        h, k = lax.rem(s, 2), lax.div(s, 2)

        for way in range(len(moves)):
            @pl.when(sends(way, k))
            def _(way=way):
                for g in range(last + 1):
                    z_copy(way, g, h, k).wait_send()

        return carry

    lax.fori_loop(0, 2 * rows, drain, 0)
    stack_copy.wait_send()
    for i in range(blocks):
        twin_copy(i).wait_send()
        for kind in range(2):
            for slot in range(cols - 1):
                left_copy(kind, i, slot).wait_send()
    for g in range(last + 1):
        twin_part(g).wait_send()
        exchange(g).wait_send()
    for g in range(last + 1):
        exchanged(g).wait_recv()


def turn(parts_ref, out_ref, held, sems):
    outs = out_ref.shape[0]
    starts = tuple(sum(GROUPS[:g]) for g in range(len(GROUPS)))
    copies = []
    for o in range(outs):
        held[o] = jnp.concatenate([
            parts_ref[side, outs * at + o * n:outs * at + (o + 1) * n]
            for side in range(2) for n, at in zip(GROUPS, starts)], axis=0).T
        if o % 4 == 3:
            part = pl.ds(o - 3, 4)
            copies.append(pltpu.make_async_copy(held.at[part], out_ref.at[part], sems.at[o]))
            copies[-1].start()
    for copy in copies:
        copy.wait()


def body(rows, cols, left_blocks, right_blocks, pair_stacks):
    left_local = left_blocks[0, 0]
    right_local = right_blocks[0, 0, 0]
    stacks = jnp.swapaxes(pair_stacks[0, 0, 0], 0, 1)
    held, sa, bs, _ = left_local.shape
    sb = right_local.shape[0]
    _, pieces, cap = stacks.shape
    outs = OUT_TILE // 2
    parts = len(GROUPS)
    tall = max(GROUPS)
    half = bs // 2
    f32 = jnp.float32
    dma = pltpu.SemaphoreType.DMA
    vmem = pl.BlockSpec(memory_space=pltpu.VMEM)
    places = pieces * cap + 1
    scratch = [
        ((held, sa, bs, bs), f32),
        ((sb, bs, bs), f32),
        ((2, pieces, sa, bs, bs), f32),
        ((2, pieces, sb * half, bs), f32),
        ((sb * half, bs), f32),
        ((2, 3, pieces, cap), jnp.int32),
        ((2, 2, pieces, bs), jnp.int32),
        ((2, 3, pieces, bs), jnp.int32),
        ((2, pieces, 2 * bs, sa * bs), jnp.bfloat16),
        ((sa * sb, tall, bs), f32),
        ((sa * sb, tall, bs), f32),
        ((places, tall, bs), f32),
        ((places, tall, bs), f32),
        ((outs * half, bs), f32),
    ]
    size = outs * bs * bs * 4
    for shape, kind in scratch:
        count = 1
        for d in shape:
            count *= d
        size += count * jnp.dtype(kind).itemsize
    refs = [pltpu.VMEM(shape, kind) for shape, kind in scratch]
    refs.insert(8, pltpu.SMEM((2, 3, pieces, bs), jnp.int32))
    result = pl.pallas_call(
        functools.partial(kernel, rows, cols),
        out_shape=jax.ShapeDtypeStruct((2, outs * half, bs), f32),
        in_specs=[pl.BlockSpec(memory_space=pltpu.HBM)] * 3,
        out_specs=vmem,
        scratch_shapes=refs + [
            dma((2, parts, 2, pieces)),
            dma((parts, 2, pieces)),
            dma((parts,)),
            dma((parts,)),
            dma((parts,)),
            dma((held * sa,)),
            dma((held * sa,)),
            dma((2, held * sa, cols - 1)),
            dma((2, held * sa, cols - 1)),
            dma, dma,
            dma((2,)),
            dma((3,)),
        ],
        compiler_params=pltpu.CompilerParams(
            collective_id=0, has_side_effects=True, vmem_limit_bytes=size + (6 << 20)),
        name="column_window",
    )(*(pltpu.with_memory_space_constraint(v, pltpu.HBM) for v in (left_local, right_local, stacks)))
    turned = pl.pallas_call(
        turn,
        out_shape=jax.ShapeDtypeStruct((outs, bs, bs), f32),
        in_specs=[vmem],
        out_specs=pl.BlockSpec(memory_space=pltpu.HBM),
        scratch_shapes=[pltpu.VMEM((outs, bs, bs), f32), dma((outs,))],
        compiler_params=pltpu.CompilerParams(vmem_limit_bytes=8 << 20),
        name="turn",
    )(result)
    return turned[None, None]


def solution(mesh):
    placed = (
        P("row", "layer", "col", None, None, None),
        P("layer", "row", "col", None, None, None),
        P("row", "col", "layer", None, None, None),
    )
    return jax.shard_map(
        functools.partial(body, mesh.shape["row"], mesh.shape["col"]),
        mesh=mesh,
        in_specs=placed,
        out_specs=P("row", "col", "layer", None, None),
        check_vma=False,
    )
```
